768 devices in a mesh: gx: 48 (over z, x), gy: 16 (over y, core).
Axes of the slice: x: 4, y: 8, z: 12, core: 2. Of those that a mesh axis runs over, the one named last changes fastest.
Arguments:
- electric: float32 [3, 1536, 256, 128], P(None, 'gx', 'gy'), may hold values from -6 to 6
- magnetic: float32 [3, 1536, 256, 128], P(None, 'gx', 'gy'), may hold values from -6 to 6
- material: int32 [1536, 256, 128], P('gx', 'gy'), may hold values from 0 to 3
- pml_flags: int32 [1536, 256, 128], P('gx', 'gy'), may hold values 0 or 1
- permittivity: float32 [4], replicated, may hold values from 1 to 12
- pml_sigma: float32 [128], replicated, may hold values from 0.05 to 1
- omega: float32 [8], replicated, may hold values from 0.5 to 3
Outputs:
- electric_out: float32 [3, 1536, 256, 128], P(None, 'gx', 'gy')
- magnetic_out: float32 [3, 1536, 256, 128], P(None, 'gx', 'gy')
- spectra: float32 [16, 2, 1536, 256], P('gy', None, 'gx')
The draws below stay inside these ranges and needn't reach their ends.
All inputs are finite; a program needn't handle non-finite values. No bound on the sum of `pml_flags` on one device may be relied on, other than what follows from the above.
Results may differ from the reference program's by a relative error of at most 0.00002.
Values sent between devices are 32-bit elements; how exact they have to be, the bound alone decides.
No kernel may reach another device: no remote copies, remote signals or barrier semaphores. Data moves between devices by JAX's collectives and lax.ppermute only.
A program may use at most 32 MiB of HBM per device.

```python
import math
import jax
import jax.numpy as jnp
from jax import lax

STEPS = 2
NFREQ = 8
NMAT = 4
NX = 1536
NY = 256
NZ = 128


def set_ends(array, rng, least, largest):
    longest = array.shape.index(max(array.shape))
    spots = []
    for shift in (0, 1):
        where = [jax.random.randint(jax.random.fold_in(rng, axis), (), 0, length) for axis, length in enumerate(array.shape)]
        where[longest] = (where[longest] + shift) % array.shape[longest]
        spots.append(tuple(where))
    return array.at[spots[0]].set(least).at[spots[1]].set(largest)


def shard_levels(own_key, shape, pieces, least, top_value):
    loudness = 1.0
    for axis_at, blocks in pieces:
        heights = jax.random.uniform(jax.random.fold_in(jax.random.fold_in(own_key, 6), axis_at), (blocks,), jnp.float32, least / len(pieces), top_value / len(pieces))
        loudness = loudness * jnp.repeat(jnp.exp(heights), shape[axis_at] // blocks).reshape((-1,) + (1,) * (len(shape) - 1 - axis_at))
    return loudness


def normal_values(key, extent, spread, limit, shards=(), dtype=jnp.bfloat16):
    entries = jax.random.normal(key, extent, jnp.float32) * spread
    if len(shards) > 0:
        entries = shard_levels(key, extent, shards, -0.22, 0.18) * entries
    return jnp.clip(entries, min=-limit, max=limit).astype(dtype)


def setup_inputs(seed: int = 0) -> dict:
    key_of = jax.random.split(jax.random.key(seed), 8)
    return {
        "electric": normal_values(key_of[0], (3, NX, NY, NZ), 1.0, 6.0, ((1, 48), (2, 16)), jnp.float32),
        "magnetic": normal_values(key_of[1], (3, NX, NY, NZ), 1.0, 6.0, ((1, 48), (2, 16)), jnp.float32),
        "material": set_ends(jax.random.randint(key_of[2], (NX, NY, NZ), 0, NMAT), jax.random.fold_in(key_of[2], 1), 0, NMAT - 1).astype(jnp.int32),
        "pml_flags": set_ends((jax.random.randint(key_of[3], (NX, NY, NZ), 0, 3) < 1).astype(jnp.int32), jax.random.fold_in(key_of[3], 1), 0, 1),
        "permittivity": jnp.clip(jnp.exp(jax.random.uniform(key_of[4], (NMAT,), jnp.float32, math.log(1.0), math.log(12.0))), 1.0, 12.0),
        "pml_sigma": jnp.clip(jnp.exp(jax.random.uniform(key_of[5], (NZ,), jnp.float32, math.log(0.05), math.log(1.0))), 0.05, 1.0),
        "omega": jnp.clip(jnp.exp(jax.random.uniform(key_of[6], (NFREQ,), jnp.float32, math.log(0.5), math.log(3.0))), 0.5, 3.0),
    }


time_step = 0.5


def forward_diff(field, axis):
    rest = lax.slice_in_dim(field, 1, field.shape[axis], axis=axis)
    edge = jnp.zeros_like(lax.slice_in_dim(field, 0, 1, axis=axis))
    return jnp.concatenate([rest, edge], axis=axis) - field


def backward_diff(field, axis):
    rest = lax.slice_in_dim(field, 0, field.shape[axis] - 1, axis=axis)
    edge = jnp.zeros_like(lax.slice_in_dim(field, 0, 1, axis=axis))
    return field - jnp.concatenate([edge, rest], axis=axis)


def reference(electric, magnetic, material, pml_flags, permittivity, pml_sigma, omega):
    eps_cell = jnp.zeros(material.shape, jnp.float32)
    for index in range(NMAT):
        eps_cell = eps_cell + (material == index).astype(jnp.float32) * permittivity[index]
    sigma_cell = pml_flags.astype(jnp.float32) * pml_sigma[None, None, :]
    s_mag = sigma_cell * time_step / 2.0
    h_keep = (1.0 - s_mag) / (1.0 + s_mag)
    h_gain = time_step / (1.0 + s_mag)
    s_ele = sigma_cell * time_step / (2.0 * eps_cell)
    e_keep = (1.0 - s_ele) / (1.0 + s_ele)
    e_gain = time_step / (eps_cell * (1.0 + s_ele))
    plane_at = electric.shape[3] // 2
    spectra = jnp.zeros((2 * NFREQ, 2, electric.shape[1], electric.shape[2]), jnp.float32)
    for step in range(STEPS):
        moment = (step + 1) * time_step
        coef = jnp.concatenate([jnp.cos(omega * moment), -jnp.sin(omega * moment)])
        ex, ey, ez = electric[0], electric[1], electric[2]
        curl_x = forward_diff(ez, 1) - forward_diff(ey, 2)
        curl_y = forward_diff(ex, 2) - forward_diff(ez, 0)
        curl_z = forward_diff(ey, 0) - forward_diff(ex, 1)
        magnetic = h_keep[None] * magnetic - h_gain[None] * jnp.stack([curl_x, curl_y, curl_z])
        hx, hy, hz = magnetic[0], magnetic[1], magnetic[2]
        curl_x = backward_diff(hz, 1) - backward_diff(hy, 2)
        curl_y = backward_diff(hx, 2) - backward_diff(hz, 0)
        curl_z = backward_diff(hy, 0) - backward_diff(hx, 1)
        electric = e_keep[None] * electric + e_gain[None] * jnp.stack([curl_x, curl_y, curl_z])
        sample = electric[0:2, :, :, plane_at]
        spectra = spectra + coef[:, None, None, None] * sample[None]
    return electric, magnetic, spectra
```

```python
import jax
import jax.numpy as jnp
from jax import lax
from jax.experimental import pallas as pl
from jax.experimental.pallas import tpu as pltpu
from jax.sharding import PartitionSpec as P

STEPS = 2
NFREQ = 8
NMAT = 4
time_step = 0.5

EX, EY, EZ, HX, HY, HZ, FL, MT = range(8)
ALL = tuple(range(8))
U_MSG = tuple((-1, f) for f in ALL) + tuple((-2, f) for f in (EX, EY, EZ, HX, HZ, FL))
D_MSG = tuple((0, f) for f in ALL) + tuple((1, f) for f in (EX, EZ))
R_MSG = tuple((-1, f) for f in ALL) + tuple((-2, f) for f in (EX, EY, EZ, HY, HZ, FL))
L_MSG = tuple((0, f) for f in ALL) + tuple((1, f) for f in (EY, EZ))


def shifted(x, axis, by):
    devices = lax.axis_size(axis)
    pairs = [(i, i + by) for i in range(devices) if 0 <= i + by < devices]
    return lax.ppermute(x, axis, pairs)


def field_plane(refs, f, x):
    e_ref, h_ref, m_ref, p_ref = refs
    if f < 3:
        return e_ref[f, x]
    if f < 6:
        return h_ref[f - 3, x]
    source = p_ref if f == FL else m_ref
    return source[x].astype(jnp.float32) + 1.0


def field_rows(refs, f, y):
    e_ref, h_ref, m_ref, p_ref = refs
    nx, ny = m_ref.shape[0], m_ref.shape[1]
    if f < 6:
        ref = e_ref if f < 3 else h_ref
        flat = ref.reshape(3 * nx * ny, 128)
        return flat[pl.ds((f % 3) * nx * ny + y, nx, stride=ny)]
    ref = p_ref if f == FL else m_ref
    return ref.reshape(nx * ny, 128)[pl.ds(y, nx, stride=ny)].astype(jnp.float32) + 1.0


def pack_rows_kernel(e_ref, h_ref, m_ref, p_ref, up_ref, down_ref):
    refs = (e_ref, h_ref, m_ref, p_ref)
    ny = m_ref.shape[1]
    for i, (at, f) in enumerate(U_MSG):
        up_ref[i] = field_rows(refs, f, ny + at)
    for i, (at, f) in enumerate(D_MSG):
        down_ref[i] = field_rows(refs, f, at)


def fill_third(third_ref, up_ref, down_ref, nx):
    flat = third_ref.reshape(8 * nx * 8, 128)
    for i, (at, f) in enumerate(U_MSG):
        flat[pl.ds(f * nx * 8 + 8 + at, nx, stride=8)] = up_ref[i]
    for i, (at, f) in enumerate(D_MSG):
        flat[pl.ds(f * nx * 8 + at, nx, stride=8)] = down_ref[i]


def pack_planes_kernel(e_ref, h_ref, m_ref, p_ref, up_ref, down_ref, right_ref, left_ref, third_ref):
    refs = (e_ref, h_ref, m_ref, p_ref)
    nx = m_ref.shape[0]
    fill_third(third_ref, up_ref, down_ref, nx)
    for message, ref, base in ((R_MSG, right_ref, nx), (L_MSG, left_ref, 0)):
        for i, (at, f) in enumerate(message):
            ref[i, 0:16] = field_plane(refs, f, base + at)
            ref[i, 16:24] = third_ref[f, base + at]


def next_y(a):
    return pltpu.roll(a, a.shape[0] - 1, 0)


def last_y(a):
    return pltpu.roll(a, 1, 0)


def window_kernel(e_ref, h_ref, m_ref, p_ref, up_ref, down_ref, right_ref, left_ref, sigma_ref, eps_ref, coef_ref,
                  eo_ref, ho_ref, part_ref, third_ref, first_ref, tile_ref):
    refs = (e_ref, h_ref, m_ref, p_ref)
    nx = m_ref.shape[0]
    fill_third(third_ref, up_ref, down_ref, nx)
    rows = (24, 128)
    lane = lax.broadcasted_iota(jnp.int32, rows, 1)
    not_last = lane != 127
    not_first = lane != 0
    sigma = sigma_ref[...]
    s_mag = sigma * time_step / 2.0
    h_keep_row = jnp.broadcast_to((1.0 - s_mag) / (1.0 + s_mag), rows)
    h_gain_row = jnp.broadcast_to(time_step / (1.0 + s_mag), rows)
    e_keep_rows, e_gain_rows, e_gain_free = [], [], []
    for k in range(NMAT):
        eps = jnp.full((1, 128), eps_ref[k], jnp.float32)
        s_ele = sigma * time_step / (2.0 * eps)
        e_keep_rows.append(jnp.broadcast_to((1.0 - s_ele) / (1.0 + s_ele), rows))
        e_gain_rows.append(jnp.broadcast_to(time_step / (eps * (1.0 + s_ele)), rows))
        e_gain_free.append(jnp.broadcast_to(time_step / eps, rows))

    def next_z(a):
        return jnp.where(not_last, pltpu.roll(a, 127, 1), 0.0)

    def last_z(a):
        return jnp.where(not_first, pltpu.roll(a, 1, 1), 0.0)

    def planes(x):
        if 0 <= x < nx:
            return [jnp.concatenate([field_plane(refs, f, x), third_ref[f, x]], axis=0) for f in ALL]
        message, ref, at = (R_MSG, right_ref, x) if x < 0 else (L_MSG, left_ref, x - nx)
        return [ref[message.index((at, f))] if (at, f) in message else None for f in ALL]

    def h_coefs(flag):
        keep = jnp.where(flag == 2.0, h_keep_row, 1.0)
        gain = jnp.where(flag == 2.0, h_gain_row, jnp.where(flag == 0.0, 0.0, time_step))
        return keep, gain

    def e_coefs(flag, code):
        m1, m2, m3 = code == 1.0, code == 2.0, code == 3.0

        def pick(table):
            return jnp.where(m1, table[0], jnp.where(m2, table[1], jnp.where(m3, table[2], table[3])))

        keep = jnp.where(flag == 2.0, pick(e_keep_rows), 1.0)
        gain = jnp.where(flag == 2.0, pick(e_gain_rows), pick(e_gain_free))
        return keep, jnp.where(code == 0.0, 0.0, gain)

    def h_step(h, e, e_next, coefs, with_x):
        keep, gain = coefs
        ex, ey, ez = e
        hx = None
        if with_x:
            hx = keep * h[0] - gain * ((next_y(ez) - ez) - (next_z(ey) - ey))
        hy = keep * h[1] - gain * ((next_z(ex) - ex) - (e_next[2] - ez))
        hz = keep * h[2] - gain * ((e_next[1] - ey) - (next_y(ex) - ex))
        return hx, hy, hz

    def e_step(e, h, h_last, coefs):
        keep, gain = coefs
        hx, hy, hz = h
        ex = keep * e[0] + gain * ((hz - last_y(hz)) - (hy - last_z(hy)))
        ey = keep * e[1] + gain * ((hx - last_z(hx)) - (hz - h_last[2]))
        ez = keep * e[2] + gain * ((hy - h_last[1]) - (hx - last_y(hx)))
        return ex, ey, ez

    here = planes(-2)
    h1_last = e1_last = h2_last = None
    hc_last = ec_last = None
    for x in range(-2, nx + 1):
        ahead = planes(x + 1)
        hc = h_coefs(here[FL])
        h1 = h_step(here[3:6], here[:3], ahead[:3], hc, x > -2)
        e1 = ec = None
        if x >= -1:
            ec = e_coefs(here[FL], here[MT])
            e1 = e_step(here[:3], h1, h1_last, ec)
            if 0 <= x < nx:
                first_ref[0, x] = e1[0][0:16]
                first_ref[1, x] = e1[1][0:16]
        if x >= 0:
            back = x - 1
            h2 = h_step(h1_last, e1_last, e1, hc_last, True)
            if back >= 0:
                e2 = e_step(e1_last, h2, h2_last, ec_last)
                for c in range(3):
                    ho_ref[c, back] = h2[c][0:16]
                    eo_ref[c, back] = e2[c][0:16]
            h2_last = h2
        here, h1_last, e1_last, hc_last, ec_last = ahead, h1, e1, hc, ec

    tile = (8, 128)
    lead = lax.broadcasted_iota(jnp.int32, tile, 1) - lax.broadcasted_iota(jnp.int32, tile, 0)
    for step, ref in enumerate((first_ref, eo_ref)):
        for low in range(8):
            total = jnp.zeros(tile, jnp.float32)
            for c in range(2):
                for high in range(nx // 8):
                    for half in range(2):
                        value = ref[c, high * 8 + low, half * 8:half * 8 + 8, :]
                        value = jnp.broadcast_to(value[:, 64:65], tile)
                        total = jnp.where(lead == (c * (nx // 8) + high) * 16 + half * 8, value, total)
            tile_ref[step, low:low + 1] = jnp.sum(total, axis=0, keepdims=True)
    for s in range(2 * NFREQ):
        part_ref[s] = coef_ref[0, s] * tile_ref[0] + coef_ref[1, s] * tile_ref[1]


def spectra_kernel(got_ref, out_ref):
    block = lax.broadcasted_iota(jnp.int32, (8, 128), 1) // 16
    for half in range(2):
        v = [got_ref[half * 8 + k] for k in range(8)]
        for bit in range(3):
            by = 1 << bit
            low_block = (block // by) % 2 == 0
            for a in range(8):
                if a & by:
                    continue
                low, high = v[a], v[a + by]
                v[a] = jnp.where(low_block, low, pltpu.roll(high, 16 * by, 1))
                v[a + by] = jnp.where(low_block, pltpu.roll(low, 128 - 16 * by, 1), high)
        for j in range(8):
            out_ref[0, j // 4, (j % 4) * 8:(j % 4) * 8 + 8, half * 128:half * 128 + 128] = v[j]


def shape(*dims):
    return jax.ShapeDtypeStruct(dims, jnp.float32)


VM = pl.BlockSpec(memory_space=pltpu.VMEM)
SM = pl.BlockSpec(memory_space=pltpu.SMEM)
LIMIT = pltpu.CompilerParams(vmem_limit_bytes=16 << 20)


def local(electric, magnetic, material, pml_flags, permittivity, pml_sigma, omega):
    nx, ny, nz = material.shape
    fields = (electric, magnetic, material, pml_flags)
    moments = jnp.arange(1, STEPS + 1, dtype=jnp.float32)[:, None] * time_step
    coef = jnp.concatenate([jnp.cos(omega[None] * moments), -jnp.sin(omega[None] * moments)], axis=1)

    up, down = pl.pallas_call(
        pack_rows_kernel,
        out_shape=(shape(len(U_MSG), nx, nz), shape(len(D_MSG), nx, nz)),
        in_specs=[VM] * 4, out_specs=(VM, VM), compiler_params=LIMIT,
    )(*fields)
    up, down = shifted(up, "gy", 1), shifted(down, "gy", -1)
    right, left = pl.pallas_call(
        pack_planes_kernel,
        out_shape=(shape(len(R_MSG), 24, nz), shape(len(L_MSG), 24, nz)),
        in_specs=[VM] * 6, out_specs=(VM, VM),
        scratch_shapes=[pltpu.VMEM((8, nx, 8, nz), jnp.float32)], compiler_params=LIMIT,
    )(*fields, up, down)
    right, left = shifted(right, "gx", 1), shifted(left, "gx", -1)
    electric_out, magnetic_out, part = pl.pallas_call(
        window_kernel,
        out_shape=(shape(3, nx, ny, nz), shape(3, nx, ny, nz), shape(2 * NFREQ, 8, 128)),
        in_specs=[VM] * 9 + [SM, SM], out_specs=(VM, VM, VM),
        scratch_shapes=[
            pltpu.VMEM((8, nx, 8, nz), jnp.float32),
            pltpu.VMEM((2, nx, ny, nz), jnp.float32),
            pltpu.VMEM((2, 8, 128), jnp.float32),
        ], compiler_params=LIMIT,
    )(*fields, up, down, right, left, pml_sigma[None], permittivity, coef)
    got = lax.all_to_all(part, "gy", split_axis=0, concat_axis=0, tiled=True)
    spectra = pl.pallas_call(
        spectra_kernel,
        out_shape=shape(1, 2, nx, 16 * ny),
        in_specs=[VM], out_specs=VM, compiler_params=LIMIT,
    )(got)
    return electric_out, magnetic_out, spectra


def solution(mesh):
    placed = (
        P(None, "gx", "gy", None),
        P(None, "gx", "gy", None),
        P("gx", "gy", None),
        P("gx", "gy", None),
        P(),
        P(),
        P(),
    )
    return jax.shard_map(
        local,
        mesh=mesh,
        in_specs=placed,
        out_specs=(P(None, "gx", "gy", None), P(None, "gx", "gy", None), P("gy", None, "gx", None)),
        check_vma=False,
    )
```

```python
import jax
import jax.numpy as jnp
from jax import lax
from jax.experimental import pallas as pl
from jax.experimental.pallas import tpu as pltpu
from jax.sharding import PartitionSpec as P

STEPS = 2
NFREQ = 8
NMAT = 4
time_step = 0.5

EX, EY, EZ, HX, HY, HZ, FL, MT = range(8)
ALL = tuple(range(8))
U_MSG = tuple((-1, f) for f in ALL) + tuple((-2, f) for f in (EX, EY, EZ, HX, HZ, FL))
D_MSG = tuple((0, f) for f in ALL) + tuple((1, f) for f in (EX, EZ))
R_MSG = tuple((-1, f) for f in ALL) + tuple((-2, f) for f in (EX, EY, EZ, HY, HZ, FL))
L_MSG = tuple((0, f) for f in ALL) + tuple((1, f) for f in (EY, EZ))


MSG = len(U_MSG)


def paired(axis, first):
    devices = lax.axis_size(axis)
    return [(i, i + 1) for i in range(first, devices - 1, 2)]


def swap_outer(x, axis):
    pairs = paired(axis, 1)
    return lax.ppermute(x, axis, pairs + [(b, a) for a, b in pairs])


def gather_inner(x, axis):
    return lax.all_gather(x, axis, axis=0, axis_index_groups=[list(p) for p in paired(axis, 0)])


def is_second(axis):
    return lax.axis_index(axis) % 2


def field_plane(refs, f, x):
    e_ref, h_ref, code_ref = refs
    if f < 3:
        return e_ref[f, x]
    if f < 6:
        return h_ref[f - 3, x]
    return code_ref[f - FL, x]


def field_rows(refs, f, y):
    e_ref, h_ref, code_ref = refs
    ref, at = (e_ref, f) if f < 3 else (h_ref, f - 3) if f < 6 else (code_ref, f - FL)
    count, nx, ny = ref.shape[0], ref.shape[1], ref.shape[2]
    return ref.reshape(count * nx * ny, 128)[pl.ds(at * nx * ny + y, nx, stride=ny)]


def load_kernel(e_hbm, h_hbm, m_hbm, p_hbm, e_ref, h_ref, code_ref, inner_ref, outer_ref, m_ref, p_ref, sems):
    copies = [
        pltpu.make_async_copy(src, dst, sems.at[i])
        for i, (src, dst) in enumerate(((e_hbm, e_ref), (h_hbm, h_ref), (m_hbm, m_ref), (p_hbm, p_ref)))
    ]
    for copy in copies:
        copy.start()
    for copy in copies:
        copy.wait()
    code_ref[0] = p_ref[...].astype(jnp.float32) + 1.0
    code_ref[1] = m_ref[...].astype(jnp.float32) + 1.0
    refs = (e_ref, h_ref, code_ref)
    ny = m_ref.shape[1]

    def pack(up_ref, down_ref):
        for i, (at, f) in enumerate(U_MSG):
            up_ref[i] = field_rows(refs, f, ny + at)
        for i, (at, f) in enumerate(D_MSG):
            down_ref[i] = field_rows(refs, f, at)

    second = is_second("gy")

    @pl.when(second == 0)
    def _():
        pack(inner_ref, outer_ref)

    @pl.when(second == 1)
    def _():
        pack(outer_ref, inner_ref)


def planes_kernel(e_ref, h_ref, code_ref, inner_got, outer_got, inner_ref, outer_ref, third_ref):
    refs = (e_ref, h_ref, code_ref)
    nx = e_ref.shape[1]
    flat = third_ref.reshape(8 * nx * 8, 128)

    def fill(up_ref, down_ref):
        for i, (at, f) in enumerate(U_MSG):
            flat[pl.ds(f * nx * 8 + 8 + at, nx, stride=8)] = up_ref[i]
        for i, (at, f) in enumerate(D_MSG):
            flat[pl.ds(f * nx * 8 + at, nx, stride=8)] = down_ref[i]

    second = is_second("gy")

    @pl.when(second == 0)
    def _():
        fill(outer_got, inner_got.at[1])

    @pl.when(second == 1)
    def _():
        fill(inner_got.at[0], outer_got)

    def pack(right_ref, left_ref):
        for message, ref, base in ((R_MSG, right_ref, nx), (L_MSG, left_ref, 0)):
            for i, (at, f) in enumerate(message):
                ref[i, 0:16] = field_plane(refs, f, base + at)
                ref[i, 16:24] = third_ref[f, base + at]

    second_x = is_second("gx")

    @pl.when(second_x == 0)
    def _():
        pack(inner_ref, outer_ref)

    @pl.when(second_x == 1)
    def _():
        pack(outer_ref, inner_ref)


def next_y(a):
    return pltpu.roll(a, a.shape[0] - 1, 0)


def last_y(a):
    return pltpu.roll(a, 1, 0)


class Window:
    def __init__(self, sigma_ref, eps_ref):
        rows = (24, 128)
        lane = lax.broadcasted_iota(jnp.int32, rows, 1)
        self.not_last = lane != 127
        self.not_first = lane != 0
        sigma = sigma_ref[...]
        s_mag = sigma * time_step / 2.0
        self.h_keep_row = jnp.broadcast_to((1.0 - s_mag) / (1.0 + s_mag), rows)
        self.h_gain_row = jnp.broadcast_to(time_step / (1.0 + s_mag), rows)
        self.e_keep_rows, self.e_gain_rows, self.e_gain_free = [], [], []
        for k in range(NMAT):
            eps = jnp.full((1, 128), eps_ref[k], jnp.float32)
            s_ele = sigma * time_step / (2.0 * eps)
            self.e_keep_rows.append(jnp.broadcast_to((1.0 - s_ele) / (1.0 + s_ele), rows))
            self.e_gain_rows.append(jnp.broadcast_to(time_step / (eps * (1.0 + s_ele)), rows))
            self.e_gain_free.append(jnp.broadcast_to(time_step / eps, rows))

    def next_z(self, a):
        return jnp.where(self.not_last[: a.shape[0]], pltpu.roll(a, 127, 1), 0.0)

    def last_z(self, a):
        return jnp.where(self.not_first[: a.shape[0]], pltpu.roll(a, 1, 1), 0.0)

    def h_coefs(self, flag):
        keep = jnp.where(flag == 2.0, self.h_keep_row, 1.0)
        gain = jnp.where(flag == 2.0, self.h_gain_row, jnp.where(flag == 0.0, 0.0, time_step))
        return keep, gain

    def e_coefs(self, flag, code):
        m1, m2, m3 = code == 1.0, code == 2.0, code == 3.0

        def pick(table):
            return jnp.where(m1, table[0], jnp.where(m2, table[1], jnp.where(m3, table[2], table[3])))

        keep = jnp.where(flag == 2.0, pick(self.e_keep_rows), 1.0)
        gain = jnp.where(flag == 2.0, pick(self.e_gain_rows), pick(self.e_gain_free))
        return keep, jnp.where(code == 0.0, 0.0, gain)

    def h_step(self, h, e, e_next, coefs, with_x):
        keep, gain = coefs
        ex, ey, ez = e
        hx = None
        if with_x:
            hx = keep * h[0] - gain * ((next_y(ez) - ez) - (self.next_z(ey) - ey))
        hy = keep * h[1] - gain * ((self.next_z(ex) - ex) - (e_next[2] - ez))
        hz = keep * h[2] - gain * ((e_next[1] - ey) - (next_y(ex) - ex))
        return hx, hy, hz

    def e_step(self, e, h, h_last, coefs, rows=24):
        keep, gain = [c[:rows] for c in coefs]
        hz_y, hx_y = last_y(h[2])[:rows], last_y(h[0])[:rows]
        hx, hy, hz = [a[:rows] for a in h]
        ex = keep * e[0][:rows] + gain * ((hz - hz_y) - (hy - self.last_z(hy)))
        ey = keep * e[1][:rows] + gain * ((hx - self.last_z(hx)) - (hz - h_last[2][:rows]))
        ez = keep * e[2][:rows] + gain * ((hy - h_last[1][:rows]) - (hx - hx_y))
        return ex, ey, ez

    def run(self, planes, first, last, keep_first_step, store, skew):
        e0, h0, hc, ec, h1, e1, h2 = {}, {}, {}, {}, {}, {}, {}

        def fetch(x):
            if x not in e0:
                p = planes(x)
                e0[x], h0[x] = p[:3], p[3:6]
                if x <= last:
                    hc[x] = self.h_coefs(p[FL])
                if first - 1 <= x <= last:
                    ec[x] = self.e_coefs(p[FL], p[MT])

        for turn in range(first - 2, last + 2 + 3 * skew):
            x = turn
            if x <= last:
                fetch(x)
                fetch(x + 1)
                h1[x] = self.h_step(h0[x], e0[x], e0[x + 1], hc[x], x > first - 2)
            x = turn - skew
            if first - 1 <= x <= last:
                e1[x] = self.e_step(e0[x], h1[x], h1[x - 1], ec[x])
                if first <= x < last:
                    keep_first_step(x, e1[x])
            x = turn - 2 * skew - 1
            if first - 1 <= x < last:
                h2[x] = self.h_step(h1[x], e1[x], e1[x + 1], hc[x], True)
            x = turn - 3 * skew - 1
            if first <= x < last:
                store(x, self.e_step(e1[x], h2[x], h2[x - 1], ec[x], 16), h2[x])


def plane_tile(fetch, xs):
    tile = (8, 128)
    lead = lax.broadcasted_iota(jnp.int32, tile, 1) - lax.broadcasted_iota(jnp.int32, tile, 0)
    row = lax.broadcasted_iota(jnp.int32, tile, 0)
    out = jnp.zeros(tile, jnp.float32)
    for low in range(8):
        total = jnp.zeros(tile, jnp.float32)
        here = [x for x in xs if x % 8 == low]
        if not here:
            continue
        for x in here:
            for c in range(2):
                for half in range(2):
                    value = jnp.broadcast_to(fetch(c, x, half)[:, 64:65], tile)
                    total = jnp.where(lead == (c * 4 + x // 8) * 16 + half * 8, value, total)
        out = jnp.where(row == low, jnp.sum(total, axis=0, keepdims=True), out)
    return out


def inner_kernel(e_ref, h_ref, code_ref, third_ref, sigma_ref, eps_ref, eo_ref, ho_ref, tile_ref, first_ref):
    refs = (e_ref, h_ref, code_ref)
    nx = e_ref.shape[1]

    def planes(x):
        return [jnp.concatenate([field_plane(refs, f, x), third_ref[f, x]], axis=0) for f in ALL]

    def keep_first_step(x, e):
        first_ref[0, x] = e[0][0:16]
        first_ref[1, x] = e[1][0:16]

    def store(x, e, h):
        for c in range(3):
            eo_ref[c, x] = e[c]
            ho_ref[c, x] = h[c][0:16]

    Window(sigma_ref, eps_ref).run(planes, 2, nx - 2, keep_first_step, store, SKEW)
    for step, ref in enumerate((first_ref, eo_ref)):
        tile_ref[step] = plane_tile(lambda c, x, half: ref[c, x, half * 8:half * 8 + 8, :], range(2, nx - 2))


def edge_kernel(e_ref, h_ref, code_ref, third_ref, inner_got, outer_got, sigma_ref, eps_ref, tile_ref, coef_ref,
                eo_ref, ho_ref, part_ref, first_ref, right_ref, left_ref):
    refs = (e_ref, h_ref, code_ref)
    nx = e_ref.shape[1]
    second = is_second("gx")

    @pl.when(second == 0)
    def _():
        right_ref[...] = outer_got[...]
        left_ref[...] = inner_got[1]

    @pl.when(second == 1)
    def _():
        right_ref[...] = inner_got[0]
        left_ref[...] = outer_got[...]

    def planes(x):
        if 0 <= x < nx:
            return [jnp.concatenate([field_plane(refs, f, x), third_ref[f, x]], axis=0) for f in ALL]
        message, ref, at = (R_MSG, right_ref, x) if x < 0 else (L_MSG, left_ref, x - nx)
        return [ref[message.index((at, f))] if (at, f) in message else None for f in ALL]

    def slot(x):
        return x if x < 2 else x - nx + 4

    def keep_first_step(x, e):
        first_ref[0, slot(x)] = e[0][0:16]
        first_ref[1, slot(x)] = e[1][0:16]

    def store(x, e, h):
        for c in range(3):
            eo_ref[c, slot(x)] = e[c]
            ho_ref[c, slot(x)] = h[c][0:16]

    window = Window(sigma_ref, eps_ref)
    window.run(planes, 0, 2, keep_first_step, store, SKEW)
    window.run(planes, nx - 2, nx, keep_first_step, store, SKEW)
    tiles = []
    for step, ref in enumerate((first_ref, eo_ref)):
        edge = plane_tile(lambda c, x, half: ref[c, slot(x), half * 8:half * 8 + 8, :], (0, 1, nx - 2, nx - 1))
        tiles.append(tile_ref[step] + edge)
    for s in range(2 * NFREQ):
        part_ref[s] = coef_ref[0, s] * tiles[0] + coef_ref[1, s] * tiles[1]


def store_kernel(ei_ref, hi_ref, ee_ref, he_ref, eo_hbm, ho_hbm, sems):
    nx = ei_ref.shape[1]
    copies = []
    for inner, edge, out in ((ei_ref, ee_ref, eo_hbm), (hi_ref, he_ref, ho_hbm)):
        copies.append((inner.at[:, 2:nx - 2], out.at[:, 2:nx - 2]))
        copies.append((edge.at[:, 0:2], out.at[:, 0:2]))
        copies.append((edge.at[:, 2:4], out.at[:, nx - 2:nx]))
    copies = [pltpu.make_async_copy(src, dst, sems.at[i]) for i, (src, dst) in enumerate(copies)]
    for copy in copies:
        copy.start()
    for copy in copies:
        copy.wait()


def spectra_kernel(got_ref, out_ref):
    block = lax.broadcasted_iota(jnp.int32, (8, 128), 1) // 16
    for half in range(2):
        v = [got_ref[half * 8 + k] for k in range(8)]
        for bit in range(3):
            by = 1 << bit
            low_block = (block // by) % 2 == 0
            for a in range(8):
                if a & by:
                    continue
                low, high = v[a], v[a + by]
                v[a] = jnp.where(low_block, low, pltpu.roll(high, 16 * by, 1))
                v[a + by] = jnp.where(low_block, pltpu.roll(low, 128 - 16 * by, 1), high)
        for j in range(8):
            out_ref[0, j // 4, (j % 4) * 8:(j % 4) * 8 + 8, half * 128:half * 128 + 128] = v[j]


def shape(*dims):
    return jax.ShapeDtypeStruct(dims, jnp.float32)


SKEW = 1
VM = pl.BlockSpec(memory_space=pltpu.VMEM)
SM = pl.BlockSpec(memory_space=pltpu.SMEM)
HBM = pl.BlockSpec(memory_space=pltpu.HBM)
LIMIT = pltpu.CompilerParams(vmem_limit_bytes=16 << 20)


def cost(flops):
    return pl.CostEstimate(flops=flops, bytes_accessed=4 << 20, transcendentals=0)


def local(electric, magnetic, material, pml_flags, permittivity, pml_sigma, omega):
    nx, ny, nz = material.shape
    moments = jnp.arange(1, STEPS + 1, dtype=jnp.float32)[:, None] * time_step
    coef = jnp.concatenate([jnp.cos(omega[None] * moments), -jnp.sin(omega[None] * moments)], axis=1)
    whole, edge = shape(3, nx, ny, nz), shape(3, 4, ny, nz)

    e, h, code, inner, outer = pl.pallas_call(
        load_kernel,
        out_shape=(whole, whole, shape(2, nx, ny, nz), shape(MSG, nx, nz), shape(MSG, nx, nz)),
        in_specs=[HBM] * 4, out_specs=(VM,) * 5,
        scratch_shapes=[
            pltpu.VMEM((nx, ny, nz), jnp.int32), pltpu.VMEM((nx, ny, nz), jnp.int32), pltpu.SemaphoreType.DMA((4,)),
        ], compiler_params=LIMIT,
    )(*(pltpu.with_memory_space_constraint(a, pltpu.HBM) for a in (electric, magnetic, material, pml_flags)))
    outer, inner = swap_outer(outer, "gy"), gather_inner(inner, "gy")
    inner, outer, third = pl.pallas_call(
        planes_kernel,
        out_shape=(shape(MSG, 24, nz), shape(MSG, 24, nz), shape(8, nx, 8, nz)),
        in_specs=[VM] * 5, out_specs=(VM,) * 3, compiler_params=LIMIT,
    )(e, h, code, inner, outer)
    outer, inner = swap_outer(outer, "gx"), gather_inner(inner, "gx")
    sigma = pml_sigma[None]
    ei, hi, tile = pl.pallas_call(
        inner_kernel,
        out_shape=(whole, whole, shape(2, 8, 128)),
        in_specs=[VM] * 5 + [SM], out_specs=(VM,) * 3,
        scratch_shapes=[pltpu.VMEM((2, nx, ny, nz), jnp.float32)], compiler_params=LIMIT,
        cost_estimate=cost(40 << 20),
    )(e, h, code, third, sigma, permittivity)
    ee, he, part = pl.pallas_call(
        edge_kernel,
        out_shape=(edge, edge, shape(2 * NFREQ, 8, 128)),
        in_specs=[VM] * 7 + [SM, VM, SM], out_specs=(VM,) * 3,
        scratch_shapes=[
            pltpu.VMEM((2, 4, ny, nz), jnp.float32),
            pltpu.VMEM((MSG, 24, nz), jnp.float32), pltpu.VMEM((MSG, 24, nz), jnp.float32),
        ], compiler_params=LIMIT,
    )(e, h, code, third, inner, outer, sigma, permittivity, tile, coef)
    got = lax.all_to_all(part, "gy", split_axis=0, concat_axis=0, tiled=True)
    electric_out, magnetic_out = pl.pallas_call(
        store_kernel,
        out_shape=(whole, whole),
        in_specs=[VM] * 4, out_specs=(HBM, HBM),
        scratch_shapes=[pltpu.SemaphoreType.DMA((6,))], compiler_params=LIMIT,
        cost_estimate=cost(4 << 20),
    )(ei, hi, ee, he)
    spectra = pl.pallas_call(
        spectra_kernel,
        out_shape=shape(1, 2, nx, 16 * ny),
        in_specs=[VM], out_specs=VM, compiler_params=LIMIT,
    )(got)
    return electric_out, magnetic_out, spectra


def solution(mesh):
    placed = (
        P(None, "gx", "gy", None),
        P(None, "gx", "gy", None),
        P("gx", "gy", None),
        P("gx", "gy", None),
        P(),
        P(),
        P(),
    )
    return jax.shard_map(
        local,
        mesh=mesh,
        in_specs=placed,
        out_specs=(P(None, "gx", "gy", None), P(None, "gx", "gy", None), P("gy", None, "gx", None)),
        check_vma=False,
    )
```

```python
import jax
import jax.numpy as jnp
from jax import lax
from jax.experimental import pallas as pl
from jax.experimental.pallas import tpu as pltpu
from jax.sharding import PartitionSpec as P

STEPS = 2
NFREQ = 8
NMAT = 4
time_step = 0.5

EX, EY, EZ, HX, HY, HZ, FL, MT = range(8)
ALL = tuple(range(8))
U_MSG = tuple((-1, f) for f in ALL) + tuple((-2, f) for f in (EX, EY, EZ, HX, HZ, FL))
D_MSG = tuple((0, f) for f in ALL) + tuple((1, f) for f in (EX, EZ))
R_MSG = tuple((-1, f) for f in ALL) + tuple((-2, f) for f in (EX, EY, EZ, HY, HZ, FL))
L_MSG = tuple((0, f) for f in ALL) + tuple((1, f) for f in (EY, EZ))


MSG = len(U_MSG)


def paired(axis, first):
    devices = lax.axis_size(axis)
    return [(i, i + 1) for i in range(first, devices - 1, 2)]


def swapped(x, axis, first):
    pairs = paired(axis, first)
    return lax.ppermute(x, axis, pairs + [(b, a) for a, b in pairs])


def gather_inner(x, axis):
    return lax.all_gather(x, axis, axis=0, axis_index_groups=[list(p) for p in paired(axis, 0)])


def is_second(axis):
    return lax.axis_index(axis) % 2


def field_plane(refs, f, x):
    e_ref, h_ref, code_ref = refs
    if f < 3:
        return e_ref[f, x]
    if f < 6:
        return h_ref[f - 3, x]
    return code_ref[f - FL, x]


def field_rows(refs, f, y):
    e_ref, h_ref, code_ref = refs
    ref, at = (e_ref, f) if f < 3 else (h_ref, f - 3) if f < 6 else (code_ref, f - FL)
    count, nx, ny = ref.shape[0], ref.shape[1], ref.shape[2]
    return ref.reshape(count * nx * ny, 128)[pl.ds(at * nx * ny + y, nx, stride=ny)]


def load_kernel(e_hbm, h_hbm, m_hbm, p_hbm, eps_hbm, sigma_hbm, omega_hbm,
                e_ref, h_ref, code_ref, inner_ref, outer_ref, table_ref, omega_ref, m_ref, p_ref, sigma_ref, eps_ref, sems):
    pairs = [(e_hbm.at[c], e_ref.at[c]) for c in range(3)] + [(h_hbm.at[c], h_ref.at[c]) for c in range(3)]
    pairs += [(m_hbm, m_ref), (p_hbm, p_ref), (eps_hbm, eps_ref), (sigma_hbm, sigma_ref), (omega_hbm, omega_ref)]
    copies = [pltpu.make_async_copy(src, dst, sems.at[i]) for i, (src, dst) in enumerate(pairs)]
    for copy in copies:
        copy.start()
    for copy in copies:
        copy.wait()
    sigma = sigma_ref[...]
    s_mag = sigma * time_step / 2.0
    table_ref[0:1] = (1.0 - s_mag) / (1.0 + s_mag)
    table_ref[1:2] = time_step / (1.0 + s_mag)
    for k in range(NMAT):
        eps = jnp.full((1, 128), eps_ref[k], jnp.float32)
        s_ele = sigma * time_step / (2.0 * eps)
        table_ref[2 + k:3 + k] = (1.0 - s_ele) / (1.0 + s_ele)
        table_ref[6 + k:7 + k] = time_step / (eps * (1.0 + s_ele))
        table_ref[10 + k:11 + k] = time_step / eps
    code_ref[0] = p_ref[...].astype(jnp.float32) + 1.0
    code_ref[1] = m_ref[...].astype(jnp.float32) + 1.0
    refs = (e_ref, h_ref, code_ref)
    ny = m_ref.shape[1]

    def pack(up_ref, down_ref):
        for i, (at, f) in enumerate(U_MSG):
            up_ref[i] = field_rows(refs, f, ny + at)
        for i, (at, f) in enumerate(D_MSG):
            down_ref[i] = field_rows(refs, f, at)

    second = is_second("gy")

    @pl.when(second == 0)
    def _():
        pack(inner_ref, outer_ref)

    @pl.when(second == 1)
    def _():
        pack(outer_ref, inner_ref)


def planes_kernel(e_ref, h_ref, code_ref, inner_got, outer_got, inner_ref, outer_ref, third_ref):
    refs = (e_ref, h_ref, code_ref)
    nx = e_ref.shape[1]
    flat = third_ref.reshape(8 * nx * 8, 128)

    def fill(up_ref, down_ref):
        for i, (at, f) in enumerate(U_MSG):
            flat[pl.ds(f * nx * 8 + 8 + at, nx, stride=8)] = up_ref[i]
        for i, (at, f) in enumerate(D_MSG):
            flat[pl.ds(f * nx * 8 + at, nx, stride=8)] = down_ref[i]

    second = is_second("gy")

    @pl.when(second == 0)
    def _():
        fill(outer_got, inner_got.at[1])

    @pl.when(second == 1)
    def _():
        fill(inner_got.at[0], outer_got)

    def pack(right_ref, left_ref):
        for message, ref, base in ((R_MSG, right_ref, nx), (L_MSG, left_ref, 0)):
            for i, (at, f) in enumerate(message):
                ref[i, 0:16] = field_plane(refs, f, base + at)
                ref[i, 16:24] = third_ref[f, base + at]

    second_x = is_second("gx")

    @pl.when(second_x == 0)
    def _():
        pack(inner_ref, outer_ref)

    @pl.when(second_x == 1)
    def _():
        pack(outer_ref, inner_ref)


def next_y(a):
    return pltpu.roll(a, a.shape[0] - 1, 0)


def last_y(a):
    return pltpu.roll(a, 1, 0)


class Window:
    def __init__(self, table_ref):
        rows = (24, 128)
        lane = lax.broadcasted_iota(jnp.int32, rows, 1)
        self.not_last = lane != 127
        self.not_first = lane != 0
        table = [jnp.broadcast_to(table_ref[k:k + 1], rows) for k in range(14)]
        self.h_keep_row, self.h_gain_row = table[:2]
        self.e_keep_rows, self.e_gain_rows, self.e_gain_free = table[2:6], table[6:10], table[10:14]

    def next_z(self, a):
        return jnp.where(self.not_last[: a.shape[0]], pltpu.roll(a, 127, 1), 0.0)

    def last_z(self, a):
        return jnp.where(self.not_first[: a.shape[0]], pltpu.roll(a, 1, 1), 0.0)

    def h_coefs(self, flag):
        keep = jnp.where(flag == 2.0, self.h_keep_row, 1.0)
        gain = jnp.where(flag == 2.0, self.h_gain_row, jnp.where(flag == 0.0, 0.0, time_step))
        return keep, gain

    def e_coefs(self, flag, code):
        m1, m2, m3 = code == 1.0, code == 2.0, code == 3.0

        def pick(table):
            return jnp.where(m1, table[0], jnp.where(m2, table[1], jnp.where(m3, table[2], table[3])))

        keep = jnp.where(flag == 2.0, pick(self.e_keep_rows), 1.0)
        gain = jnp.where(flag == 2.0, pick(self.e_gain_rows), pick(self.e_gain_free))
        return keep, jnp.where(code == 0.0, 0.0, gain)

    def h_step(self, h, e, e_next, coefs, with_x):
        keep, gain = coefs
        ex, ey, ez = e
        hx = None
        if with_x:
            hx = keep * h[0] - gain * ((next_y(ez) - ez) - (self.next_z(ey) - ey))
        hy = keep * h[1] - gain * ((self.next_z(ex) - ex) - (e_next[2] - ez))
        hz = keep * h[2] - gain * ((e_next[1] - ey) - (next_y(ex) - ex))
        return hx, hy, hz

    def e_step(self, e, h, h_last, coefs, rows=24):
        keep, gain = [c[:rows] for c in coefs]
        hz_y, hx_y = last_y(h[2])[:rows], last_y(h[0])[:rows]
        hx, hy, hz = [a[:rows] for a in h]
        ex = keep * e[0][:rows] + gain * ((hz - hz_y) - (hy - self.last_z(hy)))
        ey = keep * e[1][:rows] + gain * ((hx - self.last_z(hx)) - (hz - h_last[2][:rows]))
        ez = keep * e[2][:rows] + gain * ((hy - h_last[1][:rows]) - (hx - hx_y))
        return ex, ey, ez

    def run(self, planes, first, last, keep_first_step, store, skew):
        e0, h0, hc, ec, h1, e1, h2 = {}, {}, {}, {}, {}, {}, {}

        def fetch(x):
            if x not in e0:
                p = planes(x)
                e0[x], h0[x] = p[:3], p[3:6]
                if x <= last:
                    hc[x] = self.h_coefs(p[FL])
                if first - 1 <= x <= last:
                    ec[x] = self.e_coefs(p[FL], p[MT])

        for turn in range(first - 2, last + 2 + 3 * skew):
            x = turn
            if x <= last:
                fetch(x)
                fetch(x + 1)
                h1[x] = self.h_step(h0[x], e0[x], e0[x + 1], hc[x], x > first - 2)
            x = turn - skew
            if first - 1 <= x <= last:
                e1[x] = self.e_step(e0[x], h1[x], h1[x - 1], ec[x])
                if first <= x < last:
                    keep_first_step(x, e1[x])
            x = turn - 2 * skew - 1
            if first - 1 <= x < last:
                h2[x] = self.h_step(h1[x], e1[x], e1[x + 1], hc[x], True)
            x = turn - 3 * skew - 1
            if first <= x < last:
                store(x, self.e_step(e1[x], h2[x], h2[x - 1], ec[x], 16), h2[x])
            yield turn


def plane_tile(fetch, xs):
    tile = (8, 128)
    lead = lax.broadcasted_iota(jnp.int32, tile, 1) - lax.broadcasted_iota(jnp.int32, tile, 0)
    row = lax.broadcasted_iota(jnp.int32, tile, 0)
    out = jnp.zeros(tile, jnp.float32)
    for low in range(8):
        total = jnp.zeros(tile, jnp.float32)
        here = [x for x in xs if x % 8 == low]
        if not here:
            continue
        for x in here:
            for c in range(2):
                for half in range(2):
                    value = jnp.broadcast_to(fetch(c, x, half)[:, 64:65], tile)
                    total = jnp.where(lead == (c * 4 + x // 8) * 16 + half * 8, value, total)
        out = jnp.where(row == low, jnp.sum(total, axis=0, keepdims=True), out)
    return out


def inner_kernel(e_ref, h_ref, code_ref, third_ref, table_ref, eo_hbm, ho_hbm, tile_ref, first_ref, eo_ref, ho_ref, sems):
    refs = (e_ref, h_ref, code_ref)
    nx = e_ref.shape[1]

    def planes(x):
        return [jnp.concatenate([field_plane(refs, f, x), third_ref[f, x]], axis=0) for f in ALL]

    def keep_first_step(x, e):
        first_ref[0, x] = e[0][0:16]
        first_ref[1, x] = e[1][0:16]

    copies = []

    def store(x, e, h):
        for c in range(3):
            eo_ref[c, x] = e[c]
            ho_ref[c, x] = h[c][0:16]
        if x + 1 in CUTS:
            start = 2 if x + 1 == CUTS[0] else CUTS[CUTS.index(x + 1) - 1]
            for ref, hbm in ((eo_ref, eo_hbm), (ho_ref, ho_hbm)):
                part = pl.ds(start, x + 1 - start)
                copies.append(pltpu.make_async_copy(ref.at[:, part], hbm.at[:, part], sems.at[len(copies)]))
                copies[-1].start()

    for _ in Window(table_ref).run(planes, 2, nx - 2, keep_first_step, store, SKEW):
        pass
    for step, ref in enumerate((first_ref, eo_ref)):
        tile_ref[step] = plane_tile(lambda c, x, half: ref[c, x, half * 8:half * 8 + 8, :], range(2, nx - 2))
    for copy in copies:
        copy.wait()


def edge_kernel(e_ref, h_ref, code_ref, third_ref, inner_got, outer_got, table_ref, tile_ref, coef_ref,
                eo_ref, ho_ref, part_ref, first_ref, right_ref, left_ref):
    refs = (e_ref, h_ref, code_ref)
    nx = e_ref.shape[1]
    second = is_second("gx")

    @pl.when(second == 0)
    def _():
        right_ref[...] = outer_got[...]
        left_ref[...] = inner_got[...]

    @pl.when(second == 1)
    def _():
        right_ref[...] = inner_got[...]
        left_ref[...] = outer_got[...]

    def planes(x):
        if 0 <= x < nx:
            return [jnp.concatenate([field_plane(refs, f, x), third_ref[f, x]], axis=0) for f in ALL]
        message, ref, at = (R_MSG, right_ref, x) if x < 0 else (L_MSG, left_ref, x - nx)
        return [ref[message.index((at, f))] if (at, f) in message else None for f in ALL]

    def slot(x):
        return x if x < 2 else x - nx + 4

    def keep_first_step(x, e):
        first_ref[0, slot(x)] = e[0][0:16]
        first_ref[1, slot(x)] = e[1][0:16]

    def store(x, e, h):
        for c in range(3):
            eo_ref[c, slot(x)] = e[c]
            ho_ref[c, slot(x)] = h[c][0:16]

    window = Window(table_ref)
    for _ in zip(*(window.run(planes, at, at + 2, keep_first_step, store, EDGE_SKEW) for at in (0, nx - 2))):
        pass
    tiles = []
    for step, ref in enumerate((first_ref, eo_ref)):
        edge = plane_tile(lambda c, x, half: ref[c, slot(x), half * 8:half * 8 + 8, :], (0, 1, nx - 2, nx - 1))
        tiles.append(tile_ref[step] + edge)
    for s in range(2 * NFREQ):
        part_ref[s] = coef_ref[0, s] * tiles[0] + coef_ref[1, s] * tiles[1]


def last_kernel(got_ref, ee_ref, he_ref, _e, _h, eo_hbm, ho_hbm, spectra_hbm, out_ref, sems):
    nx = eo_hbm.shape[1]
    pairs = []
    for edge, out in ((ee_ref, eo_hbm), (he_ref, ho_hbm)):
        pairs.append((edge.at[:, 0:2], out.at[:, 0:2]))
        pairs.append((edge.at[:, 2:4], out.at[:, nx - 2:nx]))
    copies = [pltpu.make_async_copy(src, dst, sems.at[i]) for i, (src, dst) in enumerate(pairs)]
    for copy in copies:
        copy.start()
    unpack(got_ref, out_ref)
    copies.append(pltpu.make_async_copy(out_ref, spectra_hbm, sems.at[len(pairs)]))
    copies[-1].start()
    for copy in copies:
        copy.wait()


def unpack(got_ref, out_ref):
    block = lax.broadcasted_iota(jnp.int32, (8, 128), 1) // 16
    for half in range(2):
        v = [got_ref[half * 8 + k] for k in range(8)]
        for bit in range(3):
            by = 1 << bit
            low_block = (block // by) % 2 == 0
            for a in range(8):
                if a & by:
                    continue
                low, high = v[a], v[a + by]
                v[a] = jnp.where(low_block, low, pltpu.roll(high, 16 * by, 1))
                v[a + by] = jnp.where(low_block, pltpu.roll(low, 128 - 16 * by, 1), high)
        for j in range(8):
            out_ref[0, j // 4, (j % 4) * 8:(j % 4) * 8 + 8, half * 128:half * 128 + 128] = v[j]


def shape(*dims):
    return jax.ShapeDtypeStruct(dims, jnp.float32)


SKEW = 1
EDGE_SKEW = 1
CUTS = (10, 18, 26, 30)
VM = pl.BlockSpec(memory_space=pltpu.VMEM)
SM = pl.BlockSpec(memory_space=pltpu.SMEM)
HBM = pl.BlockSpec(memory_space=pltpu.HBM)
LIMIT = pltpu.CompilerParams(vmem_limit_bytes=16 << 20)


def cost(flops):
    return pl.CostEstimate(flops=flops, bytes_accessed=4 << 20, transcendentals=0)


def local(electric, magnetic, material, pml_flags, permittivity, pml_sigma, omega):
    nx, ny, nz = material.shape
    moments = jnp.arange(1, STEPS + 1, dtype=jnp.float32)[:, None] * time_step
    whole, edge = shape(3, nx, ny, nz), shape(3, 4, ny, nz)

    e, h, code, inner, outer, table, omega = pl.pallas_call(
        load_kernel,
        out_shape=(whole, whole, shape(2, nx, ny, nz), shape(MSG, nx, nz), shape(MSG, nx, nz), shape(16, nz), shape(1, NFREQ)),
        in_specs=[HBM] * 7, out_specs=(VM,) * 7,
        scratch_shapes=[
            pltpu.VMEM((nx, ny, nz), jnp.int32), pltpu.VMEM((nx, ny, nz), jnp.int32),
            pltpu.VMEM((1, nz), jnp.float32), pltpu.SMEM((NMAT,), jnp.float32), pltpu.SemaphoreType.DMA((11,)),
        ], compiler_params=LIMIT,
    )(*(pltpu.with_memory_space_constraint(a, pltpu.HBM) for a in (
        electric, magnetic, material, pml_flags, permittivity, pml_sigma[None], omega[None])))
    coef = jnp.concatenate([jnp.cos(omega * moments), -jnp.sin(omega * moments)], axis=1)
    outer, inner = swapped(outer, "gy", 1), gather_inner(inner, "gy")
    inner, outer, third = pl.pallas_call(
        planes_kernel,
        out_shape=(shape(MSG, 24, nz), shape(MSG, 24, nz), shape(8, nx, 8, nz)),
        in_specs=[VM] * 5, out_specs=(VM,) * 3, compiler_params=LIMIT,
    )(e, h, code, inner, outer)
    outer, inner = swapped(outer, "gx", 1), swapped(inner, "gx", 0)
    ei, hi, tile = pl.pallas_call(
        inner_kernel,
        out_shape=(whole, whole, shape(2, 8, 128)),
        in_specs=[VM] * 5, out_specs=(HBM, HBM, VM),
        scratch_shapes=[
            pltpu.VMEM((2, nx, ny, nz), jnp.float32), pltpu.VMEM((3, nx, ny, nz), jnp.float32),
            pltpu.VMEM((3, nx, ny, nz), jnp.float32), pltpu.SemaphoreType.DMA((2 * len(CUTS),)),
        ], compiler_params=LIMIT, cost_estimate=cost(40 << 20),
    )(e, h, code, third, table)
    ee, he, part = pl.pallas_call(
        edge_kernel,
        out_shape=(edge, edge, shape(2 * NFREQ, 8, 128)),
        in_specs=[VM] * 8 + [SM], out_specs=(VM,) * 3,
        scratch_shapes=[
            pltpu.VMEM((2, 4, ny, nz), jnp.float32),
            pltpu.VMEM((MSG, 24, nz), jnp.float32), pltpu.VMEM((MSG, 24, nz), jnp.float32),
        ], compiler_params=LIMIT,
    )(e, h, code, third, inner, outer, table, tile, coef)
    got = lax.all_to_all(part, "gy", split_axis=0, concat_axis=0, tiled=True)
    electric_out, magnetic_out, spectra = pl.pallas_call(
        last_kernel,
        out_shape=(whole, whole, shape(1, 2, nx, 16 * ny)),
        in_specs=[VM] * 3 + [HBM] * 2, out_specs=(HBM,) * 3, input_output_aliases={3: 0, 4: 1},
        scratch_shapes=[pltpu.VMEM((1, 2, nx, 16 * ny), jnp.float32), pltpu.SemaphoreType.DMA((5,))], compiler_params=LIMIT,
    )(got, ee, he, ei, hi)
    return electric_out, magnetic_out, spectra


def solution(mesh):
    placed = (
        P(None, "gx", "gy", None),
        P(None, "gx", "gy", None),
        P("gx", "gy", None),
        P("gx", "gy", None),
        P(),
        P(),
        P(),
    )
    return jax.shard_map(
        local,
        mesh=mesh,
        in_specs=placed,
        out_specs=(P(None, "gx", "gy", None), P(None, "gx", "gy", None), P("gy", None, "gx", None)),
        check_vma=False,
    )
```

```python
import jax
import jax.numpy as jnp
from jax import lax
from jax.experimental import pallas as pl
from jax.experimental.pallas import tpu as pltpu
from jax.sharding import PartitionSpec as P

STEPS = 2
NFREQ = 8
NMAT = 4
time_step = 0.5

EX, EY, EZ, HX, HY, HZ, FL, MT = range(8)
ALL = tuple(range(8))
U_MSG = tuple((-1, f) for f in ALL) + tuple((-2, f) for f in (EX, EY, EZ, HX, HZ, FL))
D_MSG = tuple((0, f) for f in ALL) + tuple((1, f) for f in (EX, EZ))
Q_Y, Q_Z, R_X, R_Y, R_Z, R_FLAG, R_GAIN = range(7)
P_Y, P_Z, L_GAIN, L_EY, L_EZ = range(5)
X_MSG = 7


MSG = len(U_MSG)


def paired(axis, first):
    devices = lax.axis_size(axis)
    return [(i, i + 1) for i in range(first, devices - 1, 2)]


def swapped(x, axis, first):
    pairs = paired(axis, first)
    return lax.ppermute(x, axis, pairs + [(b, a) for a, b in pairs])


def gather_inner(x, axis):
    return lax.all_gather(x, axis, axis=0, axis_index_groups=[list(p) for p in paired(axis, 0)])


def is_second(axis):
    return lax.axis_index(axis) % 2


def field_plane(refs, f, x):
    e_ref, h_ref, code_ref = refs
    if f < 3:
        return e_ref[f, x]
    if f < 6:
        return h_ref[f - 3, x]
    return code_ref[f - FL, x]


def field_rows(refs, f, y):
    e_ref, h_ref, code_ref = refs
    ref, at = (e_ref, f) if f < 3 else (h_ref, f - 3) if f < 6 else (code_ref, f - FL)
    count, nx, ny = ref.shape[0], ref.shape[1], ref.shape[2]
    return ref.reshape(count * nx * ny, 128)[pl.ds(at * nx * ny + y, nx, stride=ny)]


def load_kernel(e_hbm, h_hbm, m_hbm, p_hbm, eps_hbm, sigma_hbm, omega_hbm,
                e_ref, h_ref, code_ref, inner_ref, outer_ref, table_ref, omega_ref, m_ref, p_ref, sigma_ref, eps_ref, sems):
    pairs = [(e_hbm.at[c], e_ref.at[c]) for c in range(3)] + [(h_hbm.at[c], h_ref.at[c]) for c in range(3)]
    pairs += [(m_hbm, m_ref), (p_hbm, p_ref), (eps_hbm, eps_ref), (sigma_hbm, sigma_ref), (omega_hbm, omega_ref)]
    copies = [pltpu.make_async_copy(src, dst, sems.at[i]) for i, (src, dst) in enumerate(pairs)]
    for copy in copies:
        copy.start()
    for copy in copies:
        copy.wait()
    sigma = sigma_ref[...]
    s_mag = sigma * time_step / 2.0
    table_ref[0:1] = (1.0 - s_mag) / (1.0 + s_mag)
    table_ref[1:2] = time_step / (1.0 + s_mag)
    for k in range(NMAT):
        eps = jnp.full((1, 128), eps_ref[k], jnp.float32)
        s_ele = sigma * time_step / (2.0 * eps)
        table_ref[2 + k:3 + k] = (1.0 - s_ele) / (1.0 + s_ele)
        table_ref[6 + k:7 + k] = time_step / (eps * (1.0 + s_ele))
        table_ref[10 + k:11 + k] = time_step / eps
    code_ref[0] = p_ref[...].astype(jnp.float32) + 1.0
    code_ref[1] = m_ref[...].astype(jnp.float32) + 1.0
    refs = (e_ref, h_ref, code_ref)
    ny = m_ref.shape[1]

    def pack(up_ref, down_ref):
        for i, (at, f) in enumerate(U_MSG):
            up_ref[i] = field_rows(refs, f, ny + at)
        for i, (at, f) in enumerate(D_MSG):
            down_ref[i] = field_rows(refs, f, at)

    second = is_second("gy")

    @pl.when(second == 0)
    def _():
        pack(inner_ref, outer_ref)

    @pl.when(second == 1)
    def _():
        pack(outer_ref, inner_ref)


def planes_kernel(e_ref, h_ref, code_ref, inner_got, outer_got, table_ref, inner_ref, outer_ref, third_ref):
    refs = (e_ref, h_ref, code_ref)
    nx = e_ref.shape[1]
    flat = third_ref.reshape(8 * nx * 8, 128)

    def fill(up_ref, down_ref):
        for i, (at, f) in enumerate(U_MSG):
            flat[pl.ds(f * nx * 8 + 8 + at, nx, stride=8)] = up_ref[i]
        for i, (at, f) in enumerate(D_MSG):
            flat[pl.ds(f * nx * 8 + at, nx, stride=8)] = down_ref[i]

    second = is_second("gy")

    @pl.when(second == 0)
    def _():
        fill(outer_got, inner_got.at[1])

    @pl.when(second == 1)
    def _():
        fill(inner_got.at[0], outer_got)

    w = Window(table_ref)

    def planes(x):
        return [jnp.concatenate([field_plane(refs, f, x), third_ref[f, x]], axis=0) for f in ALL]

    def pack(right_ref, left_ref):
        far, near = planes(nx - 2), planes(nx - 1)
        _, hy_far, hz_far = w.h_step(far[3:6], far[:3], near[:3], w.h_coefs(far[FL]), False)
        (ex, ey, ez), (hx, hy, hz) = near[:3], near[3:6]
        keep, gain = w.h_coefs(near[FL])
        right_ref[Q_Y] = keep * hy - gain * ((w.next_z(ex) - ex) + ez)
        right_ref[Q_Z] = keep * hz + gain * (ey + (next_y(ex) - ex))
        hx = keep * hx - gain * ((next_y(ez) - ez) - (w.next_z(ey) - ey))
        keep, gain = w.e_coefs(near[FL], near[MT])
        right_ref[R_X] = keep * ex
        right_ref[R_Y] = keep * ey + gain * ((hx - w.last_z(hx)) + hz_far)
        right_ref[R_Z] = keep * ez - gain * (hy_far + (hx - last_y(hx)))
        right_ref[R_FLAG] = near[FL]
        right_ref[R_GAIN] = gain
        near, far = planes(0), planes(1)
        hx, hy, hz = w.h_step(near[3:6], near[:3], far[:3], w.h_coefs(near[FL]), True)
        keep, gain = w.e_coefs(near[FL], near[MT])
        left_ref[P_Y] = keep * near[EY] + gain * ((hx - w.last_z(hx)) - hz)
        left_ref[P_Z] = keep * near[EZ] + gain * (hy - (hx - last_y(hx)))
        left_ref[L_GAIN] = gain
        left_ref[L_EY] = near[EY]
        left_ref[L_EZ] = near[EZ]

    second_x = is_second("gx")

    @pl.when(second_x == 0)
    def _():
        pack(inner_ref, outer_ref)

    @pl.when(second_x == 1)
    def _():
        pack(outer_ref, inner_ref)


def next_y(a):
    return pltpu.roll(a, a.shape[0] - 1, 0)


def last_y(a):
    return pltpu.roll(a, 1, 0)


class Window:
    def __init__(self, table_ref):
        rows = (24, 128)
        lane = lax.broadcasted_iota(jnp.int32, rows, 1)
        self.not_last = lane != 127
        self.not_first = lane != 0
        table = [jnp.broadcast_to(table_ref[k:k + 1], rows) for k in range(14)]
        self.h_keep_row, self.h_gain_row = table[:2]
        self.e_keep_rows, self.e_gain_rows, self.e_gain_free = table[2:6], table[6:10], table[10:14]

    def next_z(self, a):
        return jnp.where(self.not_last[: a.shape[0]], pltpu.roll(a, 127, 1), 0.0)

    def last_z(self, a):
        return jnp.where(self.not_first[: a.shape[0]], pltpu.roll(a, 1, 1), 0.0)

    def h_coefs(self, flag):
        keep = jnp.where(flag == 2.0, self.h_keep_row, 1.0)
        gain = jnp.where(flag == 2.0, self.h_gain_row, jnp.where(flag == 0.0, 0.0, time_step))
        return keep, gain

    def e_coefs(self, flag, code):
        m1, m2, m3 = code == 1.0, code == 2.0, code == 3.0

        def pick(table):
            return jnp.where(m1, table[0], jnp.where(m2, table[1], jnp.where(m3, table[2], table[3])))

        keep = jnp.where(flag == 2.0, pick(self.e_keep_rows), 1.0)
        gain = jnp.where(flag == 2.0, pick(self.e_gain_rows), pick(self.e_gain_free))
        return keep, jnp.where(code == 0.0, 0.0, gain)

    def h_step(self, h, e, e_next, coefs, with_x):
        keep, gain = coefs
        ex, ey, ez = e
        hx = None
        if with_x:
            hx = keep * h[0] - gain * ((next_y(ez) - ez) - (self.next_z(ey) - ey))
        hy = keep * h[1] - gain * ((self.next_z(ex) - ex) - (e_next[2] - ez))
        hz = keep * h[2] - gain * ((e_next[1] - ey) - (next_y(ex) - ex))
        return hx, hy, hz

    def e_step(self, e, h, h_last, coefs, rows=24):
        keep, gain = [c[:rows] for c in coefs]
        hz_y, hx_y = last_y(h[2])[:rows], last_y(h[0])[:rows]
        hx, hy, hz = [a[:rows] for a in h]
        ex = keep * e[0][:rows] + gain * ((hz - hz_y) - (hy - self.last_z(hy)))
        ey = keep * e[1][:rows] + gain * ((hx - self.last_z(hx)) - (hz - h_last[2][:rows]))
        ez = keep * e[2][:rows] + gain * ((hy - h_last[1][:rows]) - (hx - hx_y))
        return ex, ey, ez

    def run(self, planes, first, last, keep_first_step, store, skew, behind=None, ahead=None):
        e0, h0, hc, ec, h1, e1, h2 = {}, {}, {}, {}, {}, {}, {}
        begin = first - 2 if behind is None else first - 1

        def fetch(x):
            if x in e0:
                return
            if ahead is not None and x == last:
                e0[x] = (None, ahead[L_EY], ahead[L_EZ])
            elif behind is not None and x < first:
                e0[x], hc[x] = None, self.h_coefs(behind[R_FLAG])
            else:
                p = planes(x)
                e0[x], h0[x] = p[:3], p[3:6]
                if x <= last:
                    hc[x] = self.h_coefs(p[FL])
                if first - 1 <= x <= last:
                    ec[x] = self.e_coefs(p[FL], p[MT])

        for turn in range(first - 2, last + 2 + 3 * skew):
            x = turn
            if begin <= x <= last - (ahead is not None):
                fetch(x)
                fetch(x + 1)
                if e0[x] is None:
                    gain = hc[x][1]
                    h1[x] = (None, behind[Q_Y] + gain * e0[x + 1][2], behind[Q_Z] - gain * e0[x + 1][1])
                else:
                    h1[x] = self.h_step(h0[x], e0[x], e0[x + 1], hc[x], x > begin or behind is not None)
            x = turn - skew
            if behind is not None and x == first - 1:
                _, hy, hz = h1[x]
                gain = behind[R_GAIN]
                ex = behind[R_X] + gain * ((hz - last_y(hz)) - (hy - self.last_z(hy)))
                e1[x] = (ex, behind[R_Y] - gain * hz, behind[R_Z] + gain * hy)
            elif ahead is not None and x == last:
                _, hy, hz = h1[x - 1]
                e1[x] = (None, ahead[P_Y] + ahead[L_GAIN] * hz, ahead[P_Z] - ahead[L_GAIN] * hy)
            elif first - 1 <= x <= last:
                e1[x] = self.e_step(e0[x], h1[x], h1[x - 1], ec[x])
                if first <= x < last:
                    keep_first_step(x, e1[x])
            x = turn - 2 * skew - 1
            if first - 1 <= x < last:
                h2[x] = self.h_step(h1[x], e1[x], e1[x + 1], hc[x], x >= first)
            x = turn - 3 * skew - 1
            if first <= x < last:
                store(x, self.e_step(e1[x], h2[x], h2[x - 1], ec[x], 16), h2[x])
            yield turn


def plane_tile(fetch, xs):
    tile = (8, 128)
    lead = lax.broadcasted_iota(jnp.int32, tile, 1) - lax.broadcasted_iota(jnp.int32, tile, 0)
    row = lax.broadcasted_iota(jnp.int32, tile, 0)
    out = jnp.zeros(tile, jnp.float32)
    for low in range(8):
        total = jnp.zeros(tile, jnp.float32)
        here = [x for x in xs if x % 8 == low]
        if not here:
            continue
        for x in here:
            for c in range(2):
                for half in range(2):
                    value = jnp.broadcast_to(fetch(c, x, half)[:, 64:65], tile)
                    total = jnp.where(lead == (c * 4 + x // 8) * 16 + half * 8, value, total)
        out = jnp.where(row == low, jnp.sum(total, axis=0, keepdims=True), out)
    return out


def inner_kernel(e_ref, h_ref, code_ref, third_ref, table_ref, eo_hbm, ho_hbm, tile_ref, first_ref, eo_ref, ho_ref, sems):
    refs = (e_ref, h_ref, code_ref)
    nx = e_ref.shape[1]

    def planes(x):
        return [jnp.concatenate([field_plane(refs, f, x), third_ref[f, x]], axis=0) for f in ALL]

    def keep_first_step(x, e):
        first_ref[0, x] = e[0][0:16]
        first_ref[1, x] = e[1][0:16]

    copies = []

    def store(x, e, h):
        for c in range(3):
            eo_ref[c, x] = e[c]
            ho_ref[c, x] = h[c][0:16]
        if x + 1 in CUTS:
            start = 2 if x + 1 == CUTS[0] else CUTS[CUTS.index(x + 1) - 1]
            for ref, hbm in ((eo_ref, eo_hbm), (ho_ref, ho_hbm)):
                part = pl.ds(start, x + 1 - start)
                copies.append(pltpu.make_async_copy(ref.at[:, part], hbm.at[:, part], sems.at[len(copies)]))
                copies[-1].start()

    for _ in Window(table_ref).run(planes, 2, nx - 2, keep_first_step, store, SKEW):
        pass
    for step, ref in enumerate((first_ref, eo_ref)):
        tile_ref[step] = plane_tile(lambda c, x, half: ref[c, x, half * 8:half * 8 + 8, :], range(2, nx - 2))
    for copy in copies:
        copy.wait()


def edge_kernel(e_ref, h_ref, code_ref, third_ref, outer_got, inner_got, table_ref, tile_ref, coef_ref,
                eo_ref, ho_ref, part_ref, first_ref, right_ref, left_ref):
    refs = (e_ref, h_ref, code_ref)
    nx = e_ref.shape[1]
    second = is_second("gx")

    @pl.when(second == 0)
    def _():
        right_ref[...] = outer_got[...]
        left_ref[...] = inner_got[...]

    @pl.when(second == 1)
    def _():
        right_ref[...] = inner_got[...]
        left_ref[...] = outer_got[...]

    def planes(x):
        return [jnp.concatenate([field_plane(refs, f, x), third_ref[f, x]], axis=0) for f in ALL]

    def slot(x):
        return x if x < 2 else x - nx + 4

    def keep_first_step(x, e):
        first_ref[0, slot(x)] = e[0][0:16]
        first_ref[1, slot(x)] = e[1][0:16]

    def store(x, e, h):
        for c in range(3):
            eo_ref[c, slot(x)] = e[c]
            ho_ref[c, slot(x)] = h[c][0:16]

    window = Window(table_ref)
    low = window.run(planes, 0, 2, keep_first_step, store, EDGE_SKEW, behind=right_ref)
    high = window.run(planes, nx - 2, nx, keep_first_step, store, EDGE_SKEW, ahead=left_ref)
    for _ in zip(low, high):
        pass
    tiles = []
    for step, ref in enumerate((first_ref, eo_ref)):
        edge = plane_tile(lambda c, x, half: ref[c, slot(x), half * 8:half * 8 + 8, :], (0, 1, nx - 2, nx - 1))
        tiles.append(tile_ref[step] + edge)
    for s in range(2 * NFREQ):
        part_ref[s] = coef_ref[0, s] * tiles[0] + coef_ref[1, s] * tiles[1]


def last_kernel(got_ref, ee_ref, he_ref, _e, _h, eo_hbm, ho_hbm, spectra_hbm, out_ref, sems):
    nx = eo_hbm.shape[1]
    pairs = []
    for edge, out in ((ee_ref, eo_hbm), (he_ref, ho_hbm)):
        pairs.append((edge.at[:, 0:2], out.at[:, 0:2]))
        pairs.append((edge.at[:, 2:4], out.at[:, nx - 2:nx]))
    copies = [pltpu.make_async_copy(src, dst, sems.at[i]) for i, (src, dst) in enumerate(pairs)]
    for copy in copies:
        copy.start()
    unpack(got_ref, out_ref)
    copies.append(pltpu.make_async_copy(out_ref, spectra_hbm, sems.at[len(pairs)]))
    copies[-1].start()
    for copy in copies:
        copy.wait()


def unpack(got_ref, out_ref):
    block = lax.broadcasted_iota(jnp.int32, (8, 128), 1) // 16
    for half in range(2):
        v = [got_ref[half * 8 + k] for k in range(8)]
        for bit in range(3):
            by = 1 << bit
            low_block = (block // by) % 2 == 0
            for a in range(8):
                if a & by:
                    continue
                low, high = v[a], v[a + by]
                v[a] = jnp.where(low_block, low, pltpu.roll(high, 16 * by, 1))
                v[a + by] = jnp.where(low_block, pltpu.roll(low, 128 - 16 * by, 1), high)
        for j in range(8):
            out_ref[0, j // 4, (j % 4) * 8:(j % 4) * 8 + 8, half * 128:half * 128 + 128] = v[j]


def shape(*dims):
    return jax.ShapeDtypeStruct(dims, jnp.float32)


SKEW = 1
EDGE_SKEW = 1
CUTS = (10, 18, 26, 30)
VM = pl.BlockSpec(memory_space=pltpu.VMEM)
SM = pl.BlockSpec(memory_space=pltpu.SMEM)
HBM = pl.BlockSpec(memory_space=pltpu.HBM)
LIMIT = pltpu.CompilerParams(vmem_limit_bytes=16 << 20)


def cost(flops):
    return pl.CostEstimate(flops=flops, bytes_accessed=4 << 20, transcendentals=0)


def local(electric, magnetic, material, pml_flags, permittivity, pml_sigma, omega):
    nx, ny, nz = material.shape
    moments = jnp.arange(1, STEPS + 1, dtype=jnp.float32)[:, None] * time_step
    whole, edge = shape(3, nx, ny, nz), shape(3, 4, ny, nz)

    e, h, code, inner, outer, table, omega = pl.pallas_call(
        load_kernel,
        out_shape=(whole, whole, shape(2, nx, ny, nz), shape(MSG, nx, nz), shape(MSG, nx, nz), shape(16, nz), shape(1, NFREQ)),
        in_specs=[HBM] * 7, out_specs=(VM,) * 7,
        scratch_shapes=[
            pltpu.VMEM((nx, ny, nz), jnp.int32), pltpu.VMEM((nx, ny, nz), jnp.int32),
            pltpu.VMEM((1, nz), jnp.float32), pltpu.SMEM((NMAT,), jnp.float32), pltpu.SemaphoreType.DMA((11,)),
        ], compiler_params=LIMIT,
    )(*(pltpu.with_memory_space_constraint(a, pltpu.HBM) for a in (
        electric, magnetic, material, pml_flags, permittivity, pml_sigma[None], omega[None])))
    coef = jnp.concatenate([jnp.cos(omega * moments), -jnp.sin(omega * moments)], axis=1)
    outer, inner = swapped(outer, "gy", 1), gather_inner(inner, "gy")
    inner, outer, third = pl.pallas_call(
        planes_kernel,
        out_shape=(shape(X_MSG, 24, nz), shape(X_MSG, 24, nz), shape(8, nx, 8, nz)),
        in_specs=[VM] * 6, out_specs=(VM,) * 3, compiler_params=LIMIT,
    )(e, h, code, inner, outer, table)
    outer, inner = swapped(outer, "gx", 1), swapped(inner, "gx", 0)
    ei, hi, tile = pl.pallas_call(
        inner_kernel,
        out_shape=(whole, whole, shape(2, 8, 128)),
        in_specs=[VM] * 5, out_specs=(HBM, HBM, VM),
        scratch_shapes=[
            pltpu.VMEM((2, nx, ny, nz), jnp.float32), pltpu.VMEM((3, nx, ny, nz), jnp.float32),
            pltpu.VMEM((3, nx, ny, nz), jnp.float32), pltpu.SemaphoreType.DMA((2 * len(CUTS),)),
        ], compiler_params=LIMIT, cost_estimate=cost(40 << 20),
    )(e, h, code, third, table)
    ee, he, part = pl.pallas_call(
        edge_kernel,
        out_shape=(edge, edge, shape(2 * NFREQ, 8, 128)),
        in_specs=[VM] * 8 + [SM], out_specs=(VM,) * 3,
        scratch_shapes=[
            pltpu.VMEM((2, 4, ny, nz), jnp.float32),
            pltpu.VMEM((X_MSG, 24, nz), jnp.float32), pltpu.VMEM((X_MSG, 24, nz), jnp.float32),
        ], compiler_params=LIMIT,
    )(e, h, code, third, outer, inner, table, tile, coef)
    got = lax.all_to_all(part, "gy", split_axis=0, concat_axis=0, tiled=True)
    electric_out, magnetic_out, spectra = pl.pallas_call(
        last_kernel,
        out_shape=(whole, whole, shape(1, 2, nx, 16 * ny)),
        in_specs=[VM] * 3 + [HBM] * 2, out_specs=(HBM,) * 3, input_output_aliases={3: 0, 4: 1},
        scratch_shapes=[pltpu.VMEM((1, 2, nx, 16 * ny), jnp.float32), pltpu.SemaphoreType.DMA((5,))], compiler_params=LIMIT,
    )(got, ee, he, ei, hi)
    return electric_out, magnetic_out, spectra


def solution(mesh):
    placed = (
        P(None, "gx", "gy", None),
        P(None, "gx", "gy", None),
        P("gx", "gy", None),
        P("gx", "gy", None),
        P(),
        P(),
        P(),
    )
    return jax.shard_map(
        local,
        mesh=mesh,
        in_specs=placed,
        out_specs=(P(None, "gx", "gy", None), P(None, "gx", "gy", None), P("gy", None, "gx", None)),
        check_vma=False,
    )
```

```python
import jax
import jax.numpy as jnp
from jax import lax
from jax.experimental import pallas as pl
from jax.experimental.pallas import tpu as pltpu
from jax.sharding import PartitionSpec as P

STEPS = 2
NFREQ = 8
NMAT = 4
time_step = 0.5

EX, EY, EZ, HX, HY, HZ, FL, MT = range(8)
ALL = tuple(range(8))
U_MSG = tuple((-1, f) for f in ALL) + tuple((-2, f) for f in (EX, EY, EZ, HX, HZ, FL))
D_MSG = tuple((0, f) for f in ALL) + tuple((1, f) for f in (EX, EZ))
Q_Y, Q_Z, R_X, R_Y, R_Z, R_FLAG, R_GAIN = range(7)
P_Y, P_Z, L_GAIN, L_EY, L_EZ = range(5)
X_MSG = 7


MSG = len(U_MSG)


def paired(axis, first):
    devices = lax.axis_size(axis)
    return [(i, i + 1) for i in range(first, devices - 1, 2)]


def swapped(x, axis, first):
    pairs = paired(axis, first)
    return lax.ppermute(x, axis, pairs + [(b, a) for a, b in pairs])


def gather_inner(x, axis):
    return lax.all_gather(x, axis, axis=0, axis_index_groups=[list(p) for p in paired(axis, 0)])


def is_second(axis):
    return lax.axis_index(axis) % 2


def field_plane(refs, f, x):
    e_ref, h_ref, m_ref, p_ref = refs
    if f < 3:
        return e_ref[f, x]
    if f < 6:
        return h_ref[f - 3, x]
    source = p_ref if f == FL else m_ref
    return source[x].astype(jnp.float32) + 1.0


def rows_kernel(e_hbm, h_hbm, m_hbm, p_hbm, eps_hbm, sigma_hbm, omega_hbm,
                inner_ref, outer_ref, table_ref, omega_ref, up_codes, down_codes, sigma_ref, eps_ref, sems):
    ny = m_hbm.shape[1]

    def fetch(up_ref, down_ref):
        pairs = []
        for ref, last in ((up_ref, ny - 1), (down_ref, 0)):
            pairs += [(e_hbm.at[:, :, last, :], ref.at[0:3]), (h_hbm.at[:, :, last, :], ref.at[3:6])]
        pairs += [
            (p_hbm.at[:, ny - 1, :], up_codes.at[0]), (m_hbm.at[:, ny - 1, :], up_codes.at[1]),
            (p_hbm.at[:, ny - 2, :], up_codes.at[2]),
            (p_hbm.at[:, 0, :], down_codes.at[0]), (m_hbm.at[:, 0, :], down_codes.at[1]),
            (e_hbm.at[:, :, ny - 2, :], up_ref.at[8:11]),
            (h_hbm.at[0, :, ny - 2, :], up_ref.at[11]), (h_hbm.at[2, :, ny - 2, :], up_ref.at[12]),
            (e_hbm.at[0, :, 1, :], down_ref.at[8]), (e_hbm.at[2, :, 1, :], down_ref.at[9]),
            (eps_hbm, eps_ref), (sigma_hbm, sigma_ref), (omega_hbm, omega_ref),
        ]
        copies = [pltpu.make_async_copy(src, dst, sems.at[i]) for i, (src, dst) in enumerate(pairs)]
        for copy in copies:
            copy.start()
        for copy in copies:
            copy.wait()
        up_ref[6:8] = up_codes[0:2].astype(jnp.float32) + 1.0
        up_ref[13] = up_codes[2].astype(jnp.float32) + 1.0
        down_ref[6:8] = down_codes[...].astype(jnp.float32) + 1.0

    second = is_second("gy")

    @pl.when(second == 0)
    def _():
        fetch(inner_ref, outer_ref)

    @pl.when(second == 1)
    def _():
        fetch(outer_ref, inner_ref)

    sigma = sigma_ref[...]
    s_mag = sigma * time_step / 2.0
    table_ref[0:1] = (1.0 - s_mag) / (1.0 + s_mag)
    table_ref[1:2] = time_step / (1.0 + s_mag)
    for k in range(NMAT):
        eps = jnp.full((1, 128), eps_ref[k], jnp.float32)
        s_ele = sigma * time_step / (2.0 * eps)
        table_ref[2 + k:3 + k] = (1.0 - s_ele) / (1.0 + s_ele)
        table_ref[6 + k:7 + k] = time_step / (eps * (1.0 + s_ele))
        table_ref[10 + k:11 + k] = time_step / eps


def planes_kernel(e_ref, h_ref, m_ref, p_ref, inner_got, outer_got, table_ref, inner_ref, outer_ref, third_ref):
    refs = (e_ref, h_ref, m_ref, p_ref)
    nx = e_ref.shape[1]
    flat = third_ref.reshape(8 * nx * 8, 128)

    def fill(up_ref, down_ref):
        for i, (at, f) in enumerate(U_MSG):
            flat[pl.ds(f * nx * 8 + 8 + at, nx, stride=8)] = up_ref[i]
        for i, (at, f) in enumerate(D_MSG):
            flat[pl.ds(f * nx * 8 + at, nx, stride=8)] = down_ref[i]

    second = is_second("gy")

    @pl.when(second == 0)
    def _():
        fill(outer_got, inner_got.at[1])

    @pl.when(second == 1)
    def _():
        fill(inner_got.at[0], outer_got)

    w = Window(table_ref)

    def planes(x):
        return [jnp.concatenate([field_plane(refs, f, x), third_ref[f, x]], axis=0) for f in ALL]

    def pack(right_ref, left_ref):
        far, near = planes(nx - 2), planes(nx - 1)
        _, hy_far, hz_far = w.h_step(far[3:6], far[:3], near[:3], w.h_coefs(far[FL]), False)
        (ex, ey, ez), (hx, hy, hz) = near[:3], near[3:6]
        keep, gain = w.h_coefs(near[FL])
        right_ref[Q_Y] = keep * hy - gain * ((w.next_z(ex) - ex) + ez)
        right_ref[Q_Z] = keep * hz + gain * (ey + (next_y(ex) - ex))
        hx = keep * hx - gain * ((next_y(ez) - ez) - (w.next_z(ey) - ey))
        keep, gain = w.e_coefs(near[FL], near[MT])
        right_ref[R_X] = keep * ex
        right_ref[R_Y] = keep * ey + gain * ((hx - w.last_z(hx)) + hz_far)
        right_ref[R_Z] = keep * ez - gain * (hy_far + (hx - last_y(hx)))
        right_ref[R_FLAG] = near[FL]
        right_ref[R_GAIN] = gain
        near, far = planes(0), planes(1)
        hx, hy, hz = w.h_step(near[3:6], near[:3], far[:3], w.h_coefs(near[FL]), True)
        keep, gain = w.e_coefs(near[FL], near[MT])
        left_ref[P_Y] = keep * near[EY] + gain * ((hx - w.last_z(hx)) - hz)
        left_ref[P_Z] = keep * near[EZ] + gain * (hy - (hx - last_y(hx)))
        left_ref[L_GAIN] = gain
        left_ref[L_EY] = near[EY]
        left_ref[L_EZ] = near[EZ]

    second_x = is_second("gx")

    @pl.when(second_x == 0)
    def _():
        pack(inner_ref, outer_ref)

    @pl.when(second_x == 1)
    def _():
        pack(outer_ref, inner_ref)


def next_y(a):
    return pltpu.roll(a, a.shape[0] - 1, 0)


def last_y(a):
    return pltpu.roll(a, 1, 0)


class Window:
    def __init__(self, table_ref):
        rows = (24, 128)
        lane = lax.broadcasted_iota(jnp.int32, rows, 1)
        self.not_last = lane != 127
        self.not_first = lane != 0
        table = [jnp.broadcast_to(table_ref[k:k + 1], rows) for k in range(14)]
        self.h_keep_row, self.h_gain_row = table[:2]
        self.e_keep_rows, self.e_gain_rows, self.e_gain_free = table[2:6], table[6:10], table[10:14]

    def next_z(self, a):
        return jnp.where(self.not_last[: a.shape[0]], pltpu.roll(a, 127, 1), 0.0)

    def last_z(self, a):
        return jnp.where(self.not_first[: a.shape[0]], pltpu.roll(a, 1, 1), 0.0)

    def h_coefs(self, flag):
        keep = jnp.where(flag == 2.0, self.h_keep_row, 1.0)
        gain = jnp.where(flag == 2.0, self.h_gain_row, jnp.where(flag == 0.0, 0.0, time_step))
        return keep, gain

    def e_coefs(self, flag, code):
        m1, m2, m3 = code == 1.0, code == 2.0, code == 3.0

        def pick(table):
            return jnp.where(m1, table[0], jnp.where(m2, table[1], jnp.where(m3, table[2], table[3])))

        keep = jnp.where(flag == 2.0, pick(self.e_keep_rows), 1.0)
        gain = jnp.where(flag == 2.0, pick(self.e_gain_rows), pick(self.e_gain_free))
        return keep, jnp.where(code == 0.0, 0.0, gain)

    def h_step(self, h, e, e_next, coefs, with_x):
        keep, gain = coefs
        ex, ey, ez = e
        hx = None
        if with_x:
            hx = keep * h[0] - gain * ((next_y(ez) - ez) - (self.next_z(ey) - ey))
        hy = keep * h[1] - gain * ((self.next_z(ex) - ex) - (e_next[2] - ez))
        hz = keep * h[2] - gain * ((e_next[1] - ey) - (next_y(ex) - ex))
        return hx, hy, hz

    def e_step(self, e, h, h_last, coefs, rows=24):
        keep, gain = [c[:rows] for c in coefs]
        hz_y, hx_y = last_y(h[2])[:rows], last_y(h[0])[:rows]
        hx, hy, hz = [a[:rows] for a in h]
        ex = keep * e[0][:rows] + gain * ((hz - hz_y) - (hy - self.last_z(hy)))
        ey = keep * e[1][:rows] + gain * ((hx - self.last_z(hx)) - (hz - h_last[2][:rows]))
        ez = keep * e[2][:rows] + gain * ((hy - h_last[1][:rows]) - (hx - hx_y))
        return ex, ey, ez

    def run(self, planes, first, last, keep_first_step, store, skew, behind=None, ahead=None):
        e0, h0, hc, ec, h1, e1, h2 = {}, {}, {}, {}, {}, {}, {}
        begin = first - 2 if behind is None else first - 1

        def fetch(x):
            if x in e0:
                return
            if ahead is not None and x == last:
                e0[x] = (None, ahead[L_EY], ahead[L_EZ])
            elif behind is not None and x < first:
                e0[x], hc[x] = None, self.h_coefs(behind[R_FLAG])
            else:
                p = planes(x)
                e0[x], h0[x] = p[:3], p[3:6]
                if x <= last:
                    hc[x] = self.h_coefs(p[FL])
                if first - 1 <= x <= last:
                    ec[x] = self.e_coefs(p[FL], p[MT])

        for turn in range(first - 2, last + 2 + 3 * skew):
            x = turn
            if begin <= x <= last - (ahead is not None):
                fetch(x)
                fetch(x + 1)
                if e0[x] is None:
                    gain = hc[x][1]
                    h1[x] = (None, behind[Q_Y] + gain * e0[x + 1][2], behind[Q_Z] - gain * e0[x + 1][1])
                else:
                    h1[x] = self.h_step(h0[x], e0[x], e0[x + 1], hc[x], x > begin or behind is not None)
            x = turn - skew
            if behind is not None and x == first - 1:
                _, hy, hz = h1[x]
                gain = behind[R_GAIN]
                ex = behind[R_X] + gain * ((hz - last_y(hz)) - (hy - self.last_z(hy)))
                e1[x] = (ex, behind[R_Y] - gain * hz, behind[R_Z] + gain * hy)
            elif ahead is not None and x == last:
                _, hy, hz = h1[x - 1]
                e1[x] = (None, ahead[P_Y] + ahead[L_GAIN] * hz, ahead[P_Z] - ahead[L_GAIN] * hy)
            elif first - 1 <= x <= last:
                e1[x] = self.e_step(e0[x], h1[x], h1[x - 1], ec[x])
                if first <= x < last:
                    keep_first_step(x, e1[x])
            x = turn - 2 * skew - 1
            if first - 1 <= x < last:
                h2[x] = self.h_step(h1[x], e1[x], e1[x + 1], hc[x], x >= first)
            x = turn - 3 * skew - 1
            if first <= x < last:
                store(x, self.e_step(e1[x], h2[x], h2[x - 1], ec[x], 16), h2[x])
            yield turn


def plane_tile(fetch, xs):
    tile = (8, 128)
    lead = lax.broadcasted_iota(jnp.int32, tile, 1) - lax.broadcasted_iota(jnp.int32, tile, 0)
    row = lax.broadcasted_iota(jnp.int32, tile, 0)
    out = jnp.zeros(tile, jnp.float32)
    for low in range(8):
        total = jnp.zeros(tile, jnp.float32)
        here = [x for x in xs if x % 8 == low]
        if not here:
            continue
        for x in here:
            for c in range(2):
                for half in range(2):
                    value = jnp.broadcast_to(fetch(c, x, half)[:, 64:65], tile)
                    total = jnp.where(lead == (c * 4 + x // 8) * 16 + half * 8, value, total)
        out = jnp.where(row == low, jnp.sum(total, axis=0, keepdims=True), out)
    return out


def inner_kernel(e_ref, h_ref, m_ref, p_ref, third_ref, table_ref, eo_hbm, ho_hbm, tile_ref, first_ref, eo_ref, ho_ref, sems):
    refs = (e_ref, h_ref, m_ref, p_ref)
    nx = e_ref.shape[1]

    def planes(x):
        return [jnp.concatenate([field_plane(refs, f, x), third_ref[f, x]], axis=0) for f in ALL]

    def keep_first_step(x, e):
        first_ref[0, x] = e[0][0:16]
        first_ref[1, x] = e[1][0:16]

    copies = []

    def store(x, e, h):
        for c in range(3):
            eo_ref[c, x] = e[c]
            ho_ref[c, x] = h[c][0:16]
        if x + 1 in CUTS:
            start = 2 if x + 1 == CUTS[0] else CUTS[CUTS.index(x + 1) - 1]
            for ref, hbm in ((eo_ref, eo_hbm), (ho_ref, ho_hbm)):
                part = pl.ds(start, x + 1 - start)
                copies.append(pltpu.make_async_copy(ref.at[:, part], hbm.at[:, part], sems.at[len(copies)]))
                copies[-1].start()

    for _ in Window(table_ref).run(planes, 2, nx - 2, keep_first_step, store, SKEW):
        pass
    for step, ref in enumerate((first_ref, eo_ref)):
        tile_ref[step] = plane_tile(lambda c, x, half: ref[c, x, half * 8:half * 8 + 8, :], range(2, nx - 2))
    for copy in copies:
        copy.wait()


def edge_kernel(e_ref, h_ref, m_ref, p_ref, third_ref, outer_got, inner_got, table_ref, tile_ref, coef_ref,
                eo_ref, ho_ref, part_ref, first_ref, right_ref, left_ref):
    refs = (e_ref, h_ref, m_ref, p_ref)
    nx = e_ref.shape[1]
    second = is_second("gx")

    @pl.when(second == 0)
    def _():
        right_ref[...] = outer_got[...]
        left_ref[...] = inner_got[...]

    @pl.when(second == 1)
    def _():
        right_ref[...] = inner_got[...]
        left_ref[...] = outer_got[...]

    def planes(x):
        return [jnp.concatenate([field_plane(refs, f, x), third_ref[f, x]], axis=0) for f in ALL]

    def slot(x):
        return x if x < 2 else x - nx + 4

    def keep_first_step(x, e):
        first_ref[0, slot(x)] = e[0][0:16]
        first_ref[1, slot(x)] = e[1][0:16]

    def store(x, e, h):
        for c in range(3):
            eo_ref[c, slot(x)] = e[c]
            ho_ref[c, slot(x)] = h[c][0:16]

    window = Window(table_ref)
    low = window.run(planes, 0, 2, keep_first_step, store, EDGE_SKEW, behind=right_ref)
    high = window.run(planes, nx - 2, nx, keep_first_step, store, EDGE_SKEW, ahead=left_ref)
    for _ in zip(low, high):
        pass
    tiles = []
    for step, ref in enumerate((first_ref, eo_ref)):
        edge = plane_tile(lambda c, x, half: ref[c, slot(x), half * 8:half * 8 + 8, :], (0, 1, nx - 2, nx - 1))
        tiles.append(tile_ref[step] + edge)
    for s in range(2 * NFREQ):
        part_ref[s] = coef_ref[0, s] * tiles[0] + coef_ref[1, s] * tiles[1]


def last_kernel(got_ref, ee_ref, he_ref, _e, _h, eo_hbm, ho_hbm, spectra_hbm, out_ref, sems):
    nx = eo_hbm.shape[1]
    pairs = []
    for edge, out in ((ee_ref, eo_hbm), (he_ref, ho_hbm)):
        pairs.append((edge.at[:, 0:2], out.at[:, 0:2]))
        pairs.append((edge.at[:, 2:4], out.at[:, nx - 2:nx]))
    copies = [pltpu.make_async_copy(src, dst, sems.at[i]) for i, (src, dst) in enumerate(pairs)]
    for copy in copies:
        copy.start()
    unpack(got_ref, out_ref)
    copies.append(pltpu.make_async_copy(out_ref, spectra_hbm, sems.at[len(pairs)]))
    copies[-1].start()
    for copy in copies:
        copy.wait()


def unpack(got_ref, out_ref):
    block = lax.broadcasted_iota(jnp.int32, (8, 128), 1) // 16
    for half in range(2):
        v = [got_ref[half * 8 + k] for k in range(8)]
        for bit in range(3):
            by = 1 << bit
            low_block = (block // by) % 2 == 0
            for a in range(8):
                if a & by:
                    continue
                low, high = v[a], v[a + by]
                v[a] = jnp.where(low_block, low, pltpu.roll(high, 16 * by, 1))
                v[a + by] = jnp.where(low_block, pltpu.roll(low, 128 - 16 * by, 1), high)
        for j in range(8):
            out_ref[0, j // 4, (j % 4) * 8:(j % 4) * 8 + 8, half * 128:half * 128 + 128] = v[j]


def shape(*dims):
    return jax.ShapeDtypeStruct(dims, jnp.float32)


SKEW = 1
EDGE_SKEW = 1
CUTS = (10, 18, 26, 30)
VM = pl.BlockSpec(memory_space=pltpu.VMEM)
SM = pl.BlockSpec(memory_space=pltpu.SMEM)
HBM = pl.BlockSpec(memory_space=pltpu.HBM)
LIMIT = pltpu.CompilerParams(vmem_limit_bytes=16 << 20)


def cost(flops):
    return pl.CostEstimate(flops=flops, bytes_accessed=4 << 20, transcendentals=0)


def local(electric, magnetic, material, pml_flags, permittivity, pml_sigma, omega):
    nx, ny, nz = material.shape
    moments = jnp.arange(1, STEPS + 1, dtype=jnp.float32)[:, None] * time_step
    whole, edge = shape(3, nx, ny, nz), shape(3, 4, ny, nz)

    fields = (electric, magnetic, material, pml_flags)
    inner, outer, table, omega = pl.pallas_call(
        rows_kernel,
        out_shape=(shape(MSG, nx, nz), shape(MSG, nx, nz), shape(16, nz), shape(1, NFREQ)),
        in_specs=[HBM] * 7, out_specs=(VM,) * 4,
        scratch_shapes=[
            pltpu.VMEM((3, nx, nz), jnp.int32), pltpu.VMEM((2, nx, nz), jnp.int32),
            pltpu.VMEM((1, nz), jnp.float32), pltpu.SMEM((NMAT,), jnp.float32), pltpu.SemaphoreType.DMA((17,)),
        ], compiler_params=LIMIT,
    )(*(pltpu.with_memory_space_constraint(a, pltpu.HBM) for a in (*fields, permittivity, pml_sigma[None], omega[None])))
    coef = jnp.concatenate([jnp.cos(omega * moments), -jnp.sin(omega * moments)], axis=1)
    outer, inner = swapped(outer, "gy", 1), gather_inner(inner, "gy")
    inner, outer, third = pl.pallas_call(
        planes_kernel,
        out_shape=(shape(X_MSG, 24, nz), shape(X_MSG, 24, nz), shape(8, nx, 8, nz)),
        in_specs=[VM] * 7, out_specs=(VM,) * 3, compiler_params=LIMIT,
    )(*fields, inner, outer, table)
    outer, inner = swapped(outer, "gx", 1), swapped(inner, "gx", 0)
    ei, hi, tile = pl.pallas_call(
        inner_kernel,
        out_shape=(whole, whole, shape(2, 8, 128)),
        in_specs=[VM] * 6, out_specs=(HBM, HBM, VM),
        scratch_shapes=[
            pltpu.VMEM((2, nx, ny, nz), jnp.float32), pltpu.VMEM((3, nx, ny, nz), jnp.float32),
            pltpu.VMEM((3, nx, ny, nz), jnp.float32), pltpu.SemaphoreType.DMA((2 * len(CUTS),)),
        ], compiler_params=LIMIT, cost_estimate=cost(40 << 20),
    )(*fields, third, table)
    ee, he, part = pl.pallas_call(
        edge_kernel,
        out_shape=(edge, edge, shape(2 * NFREQ, 8, 128)),
        in_specs=[VM] * 9 + [SM], out_specs=(VM,) * 3,
        scratch_shapes=[
            pltpu.VMEM((2, 4, ny, nz), jnp.float32),
            pltpu.VMEM((X_MSG, 24, nz), jnp.float32), pltpu.VMEM((X_MSG, 24, nz), jnp.float32),
        ], compiler_params=LIMIT,
    )(*fields, third, outer, inner, table, tile, coef)
    got = lax.all_to_all(part, "gy", split_axis=0, concat_axis=0, tiled=True)
    electric_out, magnetic_out, spectra = pl.pallas_call(
        last_kernel,
        out_shape=(whole, whole, shape(1, 2, nx, 16 * ny)),
        in_specs=[VM] * 3 + [HBM] * 2, out_specs=(HBM,) * 3, input_output_aliases={3: 0, 4: 1},
        scratch_shapes=[pltpu.VMEM((1, 2, nx, 16 * ny), jnp.float32), pltpu.SemaphoreType.DMA((5,))], compiler_params=LIMIT,
    )(got, ee, he, ei, hi)
    return electric_out, magnetic_out, spectra


def solution(mesh):
    placed = (
        P(None, "gx", "gy", None),
        P(None, "gx", "gy", None),
        P("gx", "gy", None),
        P("gx", "gy", None),
        P(),
        P(),
        P(),
    )
    return jax.shard_map(
        local,
        mesh=mesh,
        in_specs=placed,
        out_specs=(P(None, "gx", "gy", None), P(None, "gx", "gy", None), P("gy", None, "gx", None)),
        check_vma=False,
    )
```

```python
import jax
import jax.numpy as jnp
from jax import lax
from jax.experimental import pallas as pl
from jax.experimental.pallas import tpu as pltpu
from jax.sharding import PartitionSpec as P

STEPS = 2
NFREQ = 8
NMAT = 4
time_step = 0.5

EX, EY, EZ, HX, HY, HZ, FL, MT = range(8)
ALL = tuple(range(8))
U_MSG = tuple((-1, f) for f in ALL) + tuple((-2, f) for f in (EX, EY, EZ, HX, HZ, FL))
D_MSG = tuple((0, f) for f in ALL) + tuple((1, f) for f in (EX, EZ))
Q_Y, Q_Z, R_X, R_Y, R_Z, R_FLAG, R_GAIN = range(7)
P_Y, P_Z, L_GAIN, L_EY, L_EZ = range(5)
X_MSG = 7


MSG = len(U_MSG)


def paired(axis, first):
    devices = lax.axis_size(axis)
    return [(i, i + 1) for i in range(first, devices - 1, 2)]


def swapped(x, axis, first):
    pairs = paired(axis, first)
    return lax.ppermute(x, axis, pairs + [(b, a) for a, b in pairs])


def gather_inner(x, axis):
    return lax.all_gather(x, axis, axis=0, axis_index_groups=[list(p) for p in paired(axis, 0)])


def is_second(axis):
    return lax.axis_index(axis) % 2


def field_plane(refs, f, x):
    e_ref, h_ref, m_ref, p_ref = refs
    if f < 3:
        return e_ref[f, x]
    if f < 6:
        return h_ref[f - 3, x]
    source = p_ref if f == FL else m_ref
    return source[x].astype(jnp.float32) + 1.0


def rows_kernel(e_hbm, h_hbm, m_hbm, p_hbm, eps_hbm, sigma_hbm, omega_hbm,
                inner_ref, outer_ref, table_ref, omega_ref, up_codes, down_codes, sigma_ref, eps_ref, sems):
    ny = m_hbm.shape[1]

    def fetch(up_ref, down_ref):
        pairs = []
        for ref, last in ((up_ref, ny - 1), (down_ref, 0)):
            pairs += [(e_hbm.at[:, :, last, :], ref.at[0:3]), (h_hbm.at[:, :, last, :], ref.at[3:6])]
        pairs += [
            (p_hbm.at[:, ny - 1, :], up_codes.at[0]), (m_hbm.at[:, ny - 1, :], up_codes.at[1]),
            (p_hbm.at[:, ny - 2, :], up_codes.at[2]),
            (p_hbm.at[:, 0, :], down_codes.at[0]), (m_hbm.at[:, 0, :], down_codes.at[1]),
            (e_hbm.at[:, :, ny - 2, :], up_ref.at[8:11]),
            (h_hbm.at[0, :, ny - 2, :], up_ref.at[11]), (h_hbm.at[2, :, ny - 2, :], up_ref.at[12]),
            (e_hbm.at[0, :, 1, :], down_ref.at[8]), (e_hbm.at[2, :, 1, :], down_ref.at[9]),
            (eps_hbm, eps_ref), (sigma_hbm, sigma_ref), (omega_hbm, omega_ref),
        ]
        copies = [pltpu.make_async_copy(src, dst, sems.at[i]) for i, (src, dst) in enumerate(pairs)]
        for copy in copies:
            copy.start()
        for copy in copies:
            copy.wait()
        up_ref[6:8] = up_codes[0:2].astype(jnp.float32) + 1.0
        up_ref[13] = up_codes[2].astype(jnp.float32) + 1.0
        down_ref[6:8] = down_codes[...].astype(jnp.float32) + 1.0

    second = is_second("gy")

    @pl.when(second == 0)
    def _():
        fetch(inner_ref, outer_ref)

    @pl.when(second == 1)
    def _():
        fetch(outer_ref, inner_ref)

    sigma = sigma_ref[...]
    s_mag = sigma * time_step / 2.0
    table_ref[0:1] = (1.0 - s_mag) / (1.0 + s_mag)
    table_ref[1:2] = time_step / (1.0 + s_mag)
    for k in range(NMAT):
        eps = jnp.full((1, 128), eps_ref[k], jnp.float32)
        s_ele = sigma * time_step / (2.0 * eps)
        table_ref[2 + k:3 + k] = (1.0 - s_ele) / (1.0 + s_ele)
        table_ref[6 + k:7 + k] = time_step / (eps * (1.0 + s_ele))
        table_ref[10 + k:11 + k] = time_step / eps


def planes_kernel(e_ref, h_ref, m_ref, p_ref, inner_got, outer_got, table_ref, inner_ref, outer_ref, third_ref):
    refs = (e_ref, h_ref, m_ref, p_ref)
    nx = e_ref.shape[1]
    flat = third_ref.reshape(8 * nx * 8, 128)

    def fill(up_ref, down_ref):
        for i, (at, f) in enumerate(U_MSG):
            flat[pl.ds(f * nx * 8 + 8 + at, nx, stride=8)] = up_ref[i]
        for i, (at, f) in enumerate(D_MSG):
            flat[pl.ds(f * nx * 8 + at, nx, stride=8)] = down_ref[i]

    second = is_second("gy")

    @pl.when(second == 0)
    def _():
        fill(outer_got, inner_got.at[1])

    @pl.when(second == 1)
    def _():
        fill(inner_got.at[0], outer_got)

    w = Window(table_ref)

    def planes(x):
        return [jnp.concatenate([field_plane(refs, f, x), third_ref[f, x]], axis=0) for f in ALL]

    def pack(right_ref, left_ref):
        far, near = planes(nx - 2), planes(nx - 1)
        _, hy_far, hz_far = w.h_step(far[3:6], far[:3], near[:3], w.h_coefs(far[FL]), False)
        (ex, ey, ez), (hx, hy, hz) = near[:3], near[3:6]
        keep, gain = w.h_coefs(near[FL])
        right_ref[Q_Y] = keep * hy - gain * ((w.next_z(ex) - ex) + ez)
        right_ref[Q_Z] = keep * hz + gain * (ey + (next_y(ex) - ex))
        hx = keep * hx - gain * ((next_y(ez) - ez) - (w.next_z(ey) - ey))
        keep, gain = w.e_coefs(near[FL], near[MT])
        right_ref[R_X] = keep * ex
        right_ref[R_Y] = keep * ey + gain * ((hx - w.last_z(hx)) + hz_far)
        right_ref[R_Z] = keep * ez - gain * (hy_far + (hx - last_y(hx)))
        right_ref[R_FLAG] = near[FL]
        right_ref[R_GAIN] = gain
        near, far = planes(0), planes(1)
        hx, hy, hz = w.h_step(near[3:6], near[:3], far[:3], w.h_coefs(near[FL]), True)
        keep, gain = w.e_coefs(near[FL], near[MT])
        left_ref[P_Y] = keep * near[EY] + gain * ((hx - w.last_z(hx)) - hz)
        left_ref[P_Z] = keep * near[EZ] + gain * (hy - (hx - last_y(hx)))
        left_ref[L_GAIN] = gain
        left_ref[L_EY] = near[EY]
        left_ref[L_EZ] = near[EZ]

    second_x = is_second("gx")

    @pl.when(second_x == 0)
    def _():
        pack(inner_ref, outer_ref)

    @pl.when(second_x == 1)
    def _():
        pack(outer_ref, inner_ref)


def next_y(a):
    return pltpu.roll(a, a.shape[0] - 1, 0)


def last_y(a):
    return pltpu.roll(a, 1, 0)


class Window:
    def __init__(self, table_ref):
        rows = (24, 128)
        lane = lax.broadcasted_iota(jnp.int32, rows, 1)
        self.not_last = lane != 127
        self.not_first = lane != 0
        table = [jnp.broadcast_to(table_ref[k:k + 1], rows) for k in range(14)]
        self.h_keep_row, self.h_gain_row = table[:2]
        self.e_keep_rows, self.e_gain_rows, self.e_gain_free = table[2:6], table[6:10], table[10:14]

    def next_z(self, a):
        return jnp.where(self.not_last[: a.shape[0]], pltpu.roll(a, 127, 1), 0.0)

    def last_z(self, a):
        return jnp.where(self.not_first[: a.shape[0]], pltpu.roll(a, 1, 1), 0.0)

    def h_coefs(self, flag):
        keep = jnp.where(flag == 2.0, self.h_keep_row, 1.0)
        gain = jnp.where(flag == 2.0, self.h_gain_row, jnp.where(flag == 0.0, 0.0, time_step))
        return keep, gain

    def e_coefs(self, flag, code):
        m1, m2, m3 = code == 1.0, code == 2.0, code == 3.0

        def pick(table):
            return jnp.where(m1, table[0], jnp.where(m2, table[1], jnp.where(m3, table[2], table[3])))

        keep = jnp.where(flag == 2.0, pick(self.e_keep_rows), 1.0)
        gain = jnp.where(flag == 2.0, pick(self.e_gain_rows), pick(self.e_gain_free))
        return keep, jnp.where(code == 0.0, 0.0, gain)

    def h_step(self, h, e, e_next, coefs, with_x):
        keep, gain = coefs
        ex, ey, ez = e
        hx = None
        if with_x:
            hx = keep * h[0] - gain * ((next_y(ez) - ez) - (self.next_z(ey) - ey))
        hy = keep * h[1] - gain * ((self.next_z(ex) - ex) - (e_next[2] - ez))
        hz = keep * h[2] - gain * ((e_next[1] - ey) - (next_y(ex) - ex))
        return hx, hy, hz

    def e_step(self, e, h, h_last, coefs, rows=24):
        keep, gain = [c[:rows] for c in coefs]
        hz_y, hx_y = last_y(h[2])[:rows], last_y(h[0])[:rows]
        hx, hy, hz = [a[:rows] for a in h]
        ex = keep * e[0][:rows] + gain * ((hz - hz_y) - (hy - self.last_z(hy)))
        ey = keep * e[1][:rows] + gain * ((hx - self.last_z(hx)) - (hz - h_last[2][:rows]))
        ez = keep * e[2][:rows] + gain * ((hy - h_last[1][:rows]) - (hx - hx_y))
        return ex, ey, ez

    def run(self, planes, first, last, keep_first_step, store, skew, behind=None, ahead=None, known=None, save=None):
        e0, h0, hc, ec = {}, {}, {}, {}
        h1, e1, h2 = known or ({}, {}, {})

        def note(stage, x, value):
            if save is not None:
                save(stage, x, value)
            return value

        begin = first - 2 if behind is None else first - 1

        def fetch(x):
            if x in e0:
                return
            if ahead is not None and x == last:
                e0[x] = (None, ahead[L_EY], ahead[L_EZ])
            elif behind is not None and x < first:
                e0[x], hc[x] = None, self.h_coefs(behind[R_FLAG])
            else:
                p = planes(x)
                e0[x], h0[x] = p[:3], p[3:6]
                if x <= last:
                    hc[x] = self.h_coefs(p[FL])
                if first - 1 <= x <= last:
                    ec[x] = self.e_coefs(p[FL], p[MT])

        for turn in range(first - 2, last + 2 + 3 * skew):
            x = turn
            if begin <= x <= last - (ahead is not None):
                fetch(x)
                fetch(x + 1)
                if x in h1:
                    pass
                elif e0[x] is None:
                    gain = hc[x][1]
                    h1[x] = (None, behind[Q_Y] + gain * e0[x + 1][2], behind[Q_Z] - gain * e0[x + 1][1])
                else:
                    h1[x] = note(0, x, self.h_step(h0[x], e0[x], e0[x + 1], hc[x], True))
            x = turn - skew
            if behind is not None and x == first - 1:
                _, hy, hz = h1[x]
                gain = behind[R_GAIN]
                ex = behind[R_X] + gain * ((hz - last_y(hz)) - (hy - self.last_z(hy)))
                e1[x] = (ex, behind[R_Y] - gain * hz, behind[R_Z] + gain * hy)
            elif ahead is not None and x == last:
                _, hy, hz = h1[x - 1]
                e1[x] = (None, ahead[P_Y] + ahead[L_GAIN] * hz, ahead[P_Z] - ahead[L_GAIN] * hy)
            elif first - 1 <= x <= last:
                if x not in e1:
                    e1[x] = note(1, x, self.e_step(e0[x], h1[x], h1[x - 1], ec[x]))
                if first <= x < last:
                    keep_first_step(x, e1[x])
            x = turn - 2 * skew - 1
            if first - 1 <= x < last and x not in h2:
                h2[x] = note(2, x, self.h_step(h1[x], e1[x], e1[x + 1], hc[x], h1[x][0] is not None))
            x = turn - 3 * skew - 1
            if first <= x < last:
                store(x, self.e_step(e1[x], h2[x], h2[x - 1], ec[x], 16), h2[x])
            yield turn


def plane_tile(fetch, xs):
    tile = (8, 128)
    lead = lax.broadcasted_iota(jnp.int32, tile, 1) - lax.broadcasted_iota(jnp.int32, tile, 0)
    row = lax.broadcasted_iota(jnp.int32, tile, 0)
    out = jnp.zeros(tile, jnp.float32)
    for low in range(8):
        total = jnp.zeros(tile, jnp.float32)
        here = [x for x in xs if x % 8 == low]
        if not here:
            continue
        for x in here:
            for c in range(2):
                for half in range(2):
                    value = jnp.broadcast_to(fetch(c, x, half)[:, 64:65], tile)
                    total = jnp.where(lead == (c * 4 + x // 8) * 16 + half * 8, value, total)
        out = jnp.where(row == low, jnp.sum(total, axis=0, keepdims=True), out)
    return out


def saved_planes(nx):
    return [(0, 0), (1, 1), (2, 1), (0, nx - 2), (1, nx - 2), (2, nx - 3)]


def inner_kernel(e_ref, h_ref, m_ref, p_ref, third_ref, table_ref, eo_hbm, ho_hbm, tile_ref, saved_ref, first_ref, eo_ref, ho_ref, sems):
    refs = (e_ref, h_ref, m_ref, p_ref)
    nx = e_ref.shape[1]

    def planes(x):
        return [jnp.concatenate([field_plane(refs, f, x), third_ref[f, x]], axis=0) for f in ALL]

    def keep_first_step(x, e):
        first_ref[0, x] = e[0][0:16]
        first_ref[1, x] = e[1][0:16]

    copies = []

    def store(x, e, h):
        for c in range(3):
            eo_ref[c, x] = e[c]
            ho_ref[c, x] = h[c][0:16]
        if x + 1 in CUTS:
            start = 2 if x + 1 == CUTS[0] else CUTS[CUTS.index(x + 1) - 1]
            for ref, hbm in ((eo_ref, eo_hbm), (ho_ref, ho_hbm)):
                part = pl.ds(start, x + 1 - start)
                copies.append(pltpu.make_async_copy(ref.at[:, part], hbm.at[:, part], sems.at[len(copies)]))
                copies[-1].start()

    def save(stage, x, value):
        if (stage, x) in saved_planes(nx):
            for c in range(3):
                saved_ref[saved_planes(nx).index((stage, x)), c] = value[c]

    for _ in Window(table_ref).run(planes, 2, nx - 2, keep_first_step, store, SKEW, save=save):
        pass
    for step, ref in enumerate((first_ref, eo_ref)):
        tile_ref[step] = plane_tile(lambda c, x, half: ref[c, x, half * 8:half * 8 + 8, :], range(2, nx - 2))
    for copy in copies:
        copy.wait()


def edge_kernel(e_ref, h_ref, m_ref, p_ref, third_ref, outer_got, inner_got, table_ref, tile_ref, saved_ref, coef_ref,
                eo_ref, ho_ref, part_ref, first_ref, right_ref, left_ref):
    refs = (e_ref, h_ref, m_ref, p_ref)
    nx = e_ref.shape[1]
    second = is_second("gx")

    @pl.when(second == 0)
    def _():
        right_ref[...] = outer_got[...]
        left_ref[...] = inner_got[...]

    @pl.when(second == 1)
    def _():
        right_ref[...] = inner_got[...]
        left_ref[...] = outer_got[...]

    def planes(x):
        return [jnp.concatenate([field_plane(refs, f, x), third_ref[f, x]], axis=0) for f in ALL]

    def slot(x):
        return x if x < 2 else x - nx + 4

    def keep_first_step(x, e):
        first_ref[0, slot(x)] = e[0][0:16]
        first_ref[1, slot(x)] = e[1][0:16]

    def store(x, e, h):
        for c in range(3):
            eo_ref[c, slot(x)] = e[c]
            ho_ref[c, slot(x)] = h[c][0:16]

    window = Window(table_ref)
    held = [tuple(saved_ref[k, c] for c in range(3)) for k in range(6)]
    low_known = ({0: held[0], 1: None, 2: None}, {1: held[1], 2: None}, {1: held[2]})
    high_known = (
        {nx - 4: None, nx - 3: None, nx - 2: held[3]}, {nx - 3: None, nx - 2: held[4]}, {nx - 3: held[5]},
    )
    low = window.run(planes, 0, 2, keep_first_step, store, EDGE_SKEW, behind=right_ref, known=low_known)
    high = window.run(planes, nx - 2, nx, keep_first_step, store, EDGE_SKEW, ahead=left_ref, known=high_known)
    for _ in zip(low, high):
        pass
    tiles = []
    for step, ref in enumerate((first_ref, eo_ref)):
        edge = plane_tile(lambda c, x, half: ref[c, slot(x), half * 8:half * 8 + 8, :], (0, 1, nx - 2, nx - 1))
        tiles.append(tile_ref[step] + edge)
    for s in range(2 * NFREQ):
        first_coef, second_coef = (jnp.broadcast_to(coef_ref[k:k + 1, s:s + 1], (8, 128)) for k in range(2))
        part_ref[s] = first_coef * tiles[0] + second_coef * tiles[1]


def last_kernel(got_ref, ee_ref, he_ref, _e, _h, eo_hbm, ho_hbm, spectra_hbm, out_ref, sems):
    nx = eo_hbm.shape[1]
    pairs = []
    for edge, out in ((ee_ref, eo_hbm), (he_ref, ho_hbm)):
        pairs.append((edge.at[:, 0:2], out.at[:, 0:2]))
        pairs.append((edge.at[:, 2:4], out.at[:, nx - 2:nx]))
    copies = [pltpu.make_async_copy(src, dst, sems.at[i]) for i, (src, dst) in enumerate(pairs)]
    for copy in copies:
        copy.start()
    unpack(got_ref, out_ref)
    copies.append(pltpu.make_async_copy(out_ref, spectra_hbm, sems.at[len(pairs)]))
    copies[-1].start()
    for copy in copies:
        copy.wait()


def unpack(got_ref, out_ref):
    block = lax.broadcasted_iota(jnp.int32, (8, 128), 1) // 16
    for half in range(2):
        v = [got_ref[half * 8 + k] for k in range(8)]
        for bit in range(3):
            by = 1 << bit
            low_block = (block // by) % 2 == 0
            for a in range(8):
                if a & by:
                    continue
                low, high = v[a], v[a + by]
                v[a] = jnp.where(low_block, low, pltpu.roll(high, 16 * by, 1))
                v[a + by] = jnp.where(low_block, pltpu.roll(low, 128 - 16 * by, 1), high)
        for j in range(8):
            out_ref[0, j // 4, (j % 4) * 8:(j % 4) * 8 + 8, half * 128:half * 128 + 128] = v[j]


def shape(*dims):
    return jax.ShapeDtypeStruct(dims, jnp.float32)


SKEW = 1
EDGE_SKEW = 1
CUTS = (10, 18, 26, 30)
VM = pl.BlockSpec(memory_space=pltpu.VMEM)
HBM = pl.BlockSpec(memory_space=pltpu.HBM)
LIMIT = pltpu.CompilerParams(vmem_limit_bytes=16 << 20)


def cost(flops):
    return pl.CostEstimate(flops=flops, bytes_accessed=4 << 20, transcendentals=0)


def local(electric, magnetic, material, pml_flags, permittivity, pml_sigma, omega):
    nx, ny, nz = material.shape
    moments = jnp.arange(1, STEPS + 1, dtype=jnp.float32)[:, None] * time_step
    whole, edge = shape(3, nx, ny, nz), shape(3, 4, ny, nz)

    fields = (electric, magnetic, material, pml_flags)
    inner, outer, table, omega = pl.pallas_call(
        rows_kernel,
        out_shape=(shape(MSG, nx, nz), shape(MSG, nx, nz), shape(16, nz), shape(1, NFREQ)),
        in_specs=[HBM] * 7, out_specs=(VM,) * 4,
        scratch_shapes=[
            pltpu.VMEM((3, nx, nz), jnp.int32), pltpu.VMEM((2, nx, nz), jnp.int32),
            pltpu.VMEM((1, nz), jnp.float32), pltpu.SMEM((NMAT,), jnp.float32), pltpu.SemaphoreType.DMA((17,)),
        ], compiler_params=LIMIT,
    )(*(pltpu.with_memory_space_constraint(a, pltpu.HBM) for a in (*fields, permittivity, pml_sigma[None], omega[None])))
    coef = jnp.concatenate([jnp.cos(omega * moments), -jnp.sin(omega * moments)], axis=1)
    outer, inner = swapped(outer, "gy", 1), gather_inner(inner, "gy")
    inner, outer, third = pl.pallas_call(
        planes_kernel,
        out_shape=(shape(X_MSG, 24, nz), shape(X_MSG, 24, nz), shape(8, nx, 8, nz)),
        in_specs=[VM] * 7, out_specs=(VM,) * 3, compiler_params=LIMIT,
    )(*fields, inner, outer, table)
    outer, inner = swapped(outer, "gx", 1), swapped(inner, "gx", 0)
    ei, hi, tile, saved = pl.pallas_call(
        inner_kernel,
        out_shape=(whole, whole, shape(2, 8, 128), shape(6, 3, 24, nz)),
        in_specs=[VM] * 6, out_specs=(HBM, HBM, VM, VM),
        scratch_shapes=[
            pltpu.VMEM((2, nx, ny, nz), jnp.float32), pltpu.VMEM((3, nx, ny, nz), jnp.float32),
            pltpu.VMEM((3, nx, ny, nz), jnp.float32), pltpu.SemaphoreType.DMA((2 * len(CUTS),)),
        ], compiler_params=LIMIT, cost_estimate=cost(40 << 20),
    )(*fields, third, table)
    ee, he, part = pl.pallas_call(
        edge_kernel,
        out_shape=(edge, edge, shape(2 * NFREQ, 8, 128)),
        in_specs=[VM] * 11, out_specs=(VM,) * 3,
        scratch_shapes=[
            pltpu.VMEM((2, 4, ny, nz), jnp.float32),
            pltpu.VMEM((X_MSG, 24, nz), jnp.float32), pltpu.VMEM((X_MSG, 24, nz), jnp.float32),
        ], compiler_params=LIMIT,
    )(*fields, third, outer, inner, table, tile, saved, coef)
    got = lax.all_to_all(part, "gy", split_axis=0, concat_axis=0, tiled=True)
    electric_out, magnetic_out, spectra = pl.pallas_call(
        last_kernel,
        out_shape=(whole, whole, shape(1, 2, nx, 16 * ny)),
        in_specs=[VM] * 3 + [HBM] * 2, out_specs=(HBM,) * 3, input_output_aliases={3: 0, 4: 1},
        scratch_shapes=[pltpu.VMEM((1, 2, nx, 16 * ny), jnp.float32), pltpu.SemaphoreType.DMA((5,))], compiler_params=LIMIT,
    )(got, ee, he, ei, hi)
    return electric_out, magnetic_out, spectra


def solution(mesh):
    placed = (
        P(None, "gx", "gy", None),
        P(None, "gx", "gy", None),
        P("gx", "gy", None),
        P("gx", "gy", None),
        P(),
        P(),
        P(),
    )
    return jax.shard_map(
        local,
        mesh=mesh,
        in_specs=placed,
        out_specs=(P(None, "gx", "gy", None), P(None, "gx", "gy", None), P("gy", None, "gx", None)),
        check_vma=False,
    )
```

```python
import jax
import jax.numpy as jnp
from jax import lax
from jax.experimental import pallas as pl
from jax.experimental.pallas import tpu as pltpu
from jax.sharding import PartitionSpec as P

STEPS = 2
NFREQ = 8
NMAT = 4
time_step = 0.5

EX, EY, EZ, HX, HY, HZ, FL, MT = range(8)
ALL = tuple(range(8))
U_MSG = tuple((-1, f) for f in ALL) + tuple((-2, f) for f in (EX, EY, EZ, HX, HZ, FL))
D_MSG = tuple((0, f) for f in ALL) + tuple((1, f) for f in (EX, EZ))
Q_Y, Q_Z, R_X, R_Y, R_Z, R_FLAG, R_GAIN = range(7)
P_Y, P_Z, L_GAIN, L_EY, L_EZ = range(5)
X_MSG = 7


MSG = len(U_MSG)


def paired(axis, first):
    devices = lax.axis_size(axis)
    return [(i, i + 1) for i in range(first, devices - 1, 2)]


def swapped(x, axis, first):
    pairs = paired(axis, first)
    return lax.ppermute(x, axis, pairs + [(b, a) for a, b in pairs])


def gather_inner(x, axis):
    return lax.all_gather(x, axis, axis=0, axis_index_groups=[list(p) for p in paired(axis, 0)])


def is_second(axis):
    return lax.axis_index(axis) % 2


def field_plane(refs, f, x):
    e_ref, h_ref, m_ref, p_ref = refs
    if f < 3:
        return e_ref[f, x]
    if f < 6:
        return h_ref[f - 3, x]
    source = p_ref if f == FL else m_ref
    return source[x].astype(jnp.float32) + 1.0


def rows_kernel(e_hbm, h_hbm, m_hbm, p_hbm, eps_hbm, sigma_hbm, omega_hbm,
                inner_ref, outer_ref, table_ref, omega_ref, up_codes, down_codes, sigma_ref, eps_ref, sems):
    ny = m_hbm.shape[1]

    def make_tables():
        sigma = sigma_ref[...]
        s_mag = sigma * time_step / 2.0
        table_ref[0:1] = (1.0 - s_mag) / (1.0 + s_mag)
        table_ref[1:2] = time_step / (1.0 + s_mag)
        for k in range(NMAT):
            eps = jnp.full((1, 128), eps_ref[k], jnp.float32)
            s_ele = sigma * time_step / (2.0 * eps)
            table_ref[2 + k:3 + k] = (1.0 - s_ele) / (1.0 + s_ele)
            table_ref[6 + k:7 + k] = time_step / (eps * (1.0 + s_ele))
            table_ref[10 + k:11 + k] = time_step / eps

    def fetch(up_ref, down_ref):
        pairs = [(eps_hbm, eps_ref), (sigma_hbm, sigma_ref)]
        for ref, last in ((up_ref, ny - 1), (down_ref, 0)):
            pairs += [(e_hbm.at[:, :, last, :], ref.at[0:3]), (h_hbm.at[:, :, last, :], ref.at[3:6])]
        pairs += [
            (p_hbm.at[:, ny - 1, :], up_codes.at[0]), (m_hbm.at[:, ny - 1, :], up_codes.at[1]),
            (p_hbm.at[:, ny - 2, :], up_codes.at[2]),
            (p_hbm.at[:, 0, :], down_codes.at[0]), (m_hbm.at[:, 0, :], down_codes.at[1]),
            (e_hbm.at[:, :, ny - 2, :], up_ref.at[8:11]),
            (h_hbm.at[0, :, ny - 2, :], up_ref.at[11]), (h_hbm.at[2, :, ny - 2, :], up_ref.at[12]),
            (e_hbm.at[0, :, 1, :], down_ref.at[8]), (e_hbm.at[2, :, 1, :], down_ref.at[9]),
            (omega_hbm, omega_ref),
        ]
        copies = [pltpu.make_async_copy(src, dst, sems.at[i]) for i, (src, dst) in enumerate(pairs)]
        for copy in copies:
            copy.start()
        for copy in copies[:2]:
            copy.wait()
        make_tables()
        for copy in copies[2:]:
            copy.wait()
        up_ref[6:8] = up_codes[0:2].astype(jnp.float32) + 1.0
        up_ref[13] = up_codes[2].astype(jnp.float32) + 1.0
        down_ref[6:8] = down_codes[...].astype(jnp.float32) + 1.0

    second = is_second("gy")

    @pl.when(second == 0)
    def _():
        fetch(inner_ref, outer_ref)

    @pl.when(second == 1)
    def _():
        fetch(outer_ref, inner_ref)


def planes_kernel(e_ref, h_ref, m_ref, p_ref, inner_got, outer_got, table_ref, inner_ref, outer_ref, third_ref):
    refs = (e_ref, h_ref, m_ref, p_ref)
    nx = e_ref.shape[1]
    flat = third_ref.reshape(8 * nx * 8, 128)

    def fill(up_ref, down_ref):
        for i, (at, f) in enumerate(U_MSG):
            flat[pl.ds(f * nx * 8 + 8 + at, nx, stride=8)] = up_ref[i]
        for i, (at, f) in enumerate(D_MSG):
            flat[pl.ds(f * nx * 8 + at, nx, stride=8)] = down_ref[i]

    second = is_second("gy")

    @pl.when(second == 0)
    def _():
        fill(outer_got, inner_got.at[1])

    @pl.when(second == 1)
    def _():
        fill(inner_got.at[0], outer_got)

    w = Window(table_ref)

    def planes(x):
        return [jnp.concatenate([field_plane(refs, f, x), third_ref[f, x]], axis=0) for f in ALL]

    def pack(right_ref, left_ref):
        far, near = planes(nx - 2), planes(nx - 1)
        _, hy_far, hz_far = w.h_step(far[3:6], far[:3], near[:3], w.h_coefs(far[FL]), False)
        (ex, ey, ez), (hx, hy, hz) = near[:3], near[3:6]
        keep, gain = w.h_coefs(near[FL])
        right_ref[Q_Y] = keep * hy - gain * ((w.next_z(ex) - ex) + ez)
        right_ref[Q_Z] = keep * hz + gain * (ey + (next_y(ex) - ex))
        hx = keep * hx - gain * ((next_y(ez) - ez) - (w.next_z(ey) - ey))
        keep, gain = w.e_coefs(near[FL], near[MT])
        right_ref[R_X] = keep * ex
        right_ref[R_Y] = keep * ey + gain * ((hx - w.last_z(hx)) + hz_far)
        right_ref[R_Z] = keep * ez - gain * (hy_far + (hx - last_y(hx)))
        right_ref[R_FLAG] = near[FL]
        right_ref[R_GAIN] = gain
        near, far = planes(0), planes(1)
        hx, hy, hz = w.h_step(near[3:6], near[:3], far[:3], w.h_coefs(near[FL]), True)
        keep, gain = w.e_coefs(near[FL], near[MT])
        left_ref[P_Y] = keep * near[EY] + gain * ((hx - w.last_z(hx)) - hz)
        left_ref[P_Z] = keep * near[EZ] + gain * (hy - (hx - last_y(hx)))
        left_ref[L_GAIN] = gain
        left_ref[L_EY] = near[EY]
        left_ref[L_EZ] = near[EZ]

    second_x = is_second("gx")

    @pl.when(second_x == 0)
    def _():
        pack(inner_ref, outer_ref)

    @pl.when(second_x == 1)
    def _():
        pack(outer_ref, inner_ref)


def next_y(a):
    return pltpu.roll(a, a.shape[0] - 1, 0)


def last_y(a):
    return pltpu.roll(a, 1, 0)


class Window:
    def __init__(self, table_ref):
        rows = (24, 128)
        lane = lax.broadcasted_iota(jnp.int32, rows, 1)
        self.not_last = lane != 127
        self.not_first = lane != 0
        table = [jnp.broadcast_to(table_ref[k:k + 1], rows) for k in range(14)]
        self.h_keep_row, self.h_gain_row = table[:2]
        self.e_keep_rows, self.e_gain_rows, self.e_gain_free = table[2:6], table[6:10], table[10:14]

    def next_z(self, a):
        return jnp.where(self.not_last[: a.shape[0]], pltpu.roll(a, 127, 1), 0.0)

    def last_z(self, a):
        return jnp.where(self.not_first[: a.shape[0]], pltpu.roll(a, 1, 1), 0.0)

    def h_coefs(self, flag):
        keep = jnp.where(flag == 2.0, self.h_keep_row, 1.0)
        gain = jnp.where(flag == 2.0, self.h_gain_row, jnp.where(flag == 0.0, 0.0, time_step))
        return keep, gain

    def e_coefs(self, flag, code):
        m1, m2, m3 = code == 1.0, code == 2.0, code == 3.0

        def pick(table):
            return jnp.where(m1, table[0], jnp.where(m2, table[1], jnp.where(m3, table[2], table[3])))

        keep = jnp.where(flag == 2.0, pick(self.e_keep_rows), 1.0)
        gain = jnp.where(flag == 2.0, pick(self.e_gain_rows), pick(self.e_gain_free))
        return keep, jnp.where(code == 0.0, 0.0, gain)

    def h_step(self, h, e, e_next, coefs, with_x):
        keep, gain = coefs
        ex, ey, ez = e
        hx = None
        if with_x:
            hx = keep * h[0] - gain * ((next_y(ez) - ez) - (self.next_z(ey) - ey))
        hy = keep * h[1] - gain * ((self.next_z(ex) - ex) - (e_next[2] - ez))
        hz = keep * h[2] - gain * ((e_next[1] - ey) - (next_y(ex) - ex))
        return hx, hy, hz

    def e_step(self, e, h, h_last, coefs, rows=24):
        keep, gain = [c[:rows] for c in coefs]
        hz_y, hx_y = last_y(h[2])[:rows], last_y(h[0])[:rows]
        hx, hy, hz = [a[:rows] for a in h]
        ex = keep * e[0][:rows] + gain * ((hz - hz_y) - (hy - self.last_z(hy)))
        ey = keep * e[1][:rows] + gain * ((hx - self.last_z(hx)) - (hz - h_last[2][:rows]))
        ez = keep * e[2][:rows] + gain * ((hy - h_last[1][:rows]) - (hx - hx_y))
        return ex, ey, ez

    def run(self, planes, first, last, keep_first_step, store, skew, behind=None, ahead=None, known=None, save=None):
        e0, h0, hc, ec = {}, {}, {}, {}
        h1, e1, h2 = known or ({}, {}, {})

        def note(stage, x, value):
            if save is not None:
                save(stage, x, value)
            return value

        begin = first - 2 if behind is None else first - 1

        def fetch(x):
            if x in e0:
                return
            if ahead is not None and x == last:
                e0[x] = (None, ahead[L_EY], ahead[L_EZ])
            elif behind is not None and x < first:
                e0[x], hc[x] = None, self.h_coefs(behind[R_FLAG])
            else:
                p = planes(x)
                e0[x], h0[x] = p[:3], p[3:6]
                if x <= last:
                    hc[x] = self.h_coefs(p[FL])
                if first - 1 <= x <= last:
                    ec[x] = self.e_coefs(p[FL], p[MT])

        for turn in range(first - 2, last + 2 + 3 * skew):
            x = turn
            if begin <= x <= last - (ahead is not None):
                fetch(x)
                fetch(x + 1)
                if x in h1:
                    pass
                elif e0[x] is None:
                    gain = hc[x][1]
                    h1[x] = (None, behind[Q_Y] + gain * e0[x + 1][2], behind[Q_Z] - gain * e0[x + 1][1])
                else:
                    h1[x] = note(0, x, self.h_step(h0[x], e0[x], e0[x + 1], hc[x], True))
            x = turn - skew
            if behind is not None and x == first - 1:
                _, hy, hz = h1[x]
                gain = behind[R_GAIN]
                ex = behind[R_X] + gain * ((hz - last_y(hz)) - (hy - self.last_z(hy)))
                e1[x] = (ex, behind[R_Y] - gain * hz, behind[R_Z] + gain * hy)
            elif ahead is not None and x == last:
                _, hy, hz = h1[x - 1]
                e1[x] = (None, ahead[P_Y] + ahead[L_GAIN] * hz, ahead[P_Z] - ahead[L_GAIN] * hy)
            elif first - 1 <= x <= last:
                if x not in e1:
                    e1[x] = note(1, x, self.e_step(e0[x], h1[x], h1[x - 1], ec[x]))
                if first <= x < last:
                    keep_first_step(x, e1[x])
            x = turn - 2 * skew - 1
            if first - 1 <= x < last and x not in h2:
                h2[x] = note(2, x, self.h_step(h1[x], e1[x], e1[x + 1], hc[x], h1[x][0] is not None))
            x = turn - 3 * skew - 1
            if first <= x < last:
                store(x, self.e_step(e1[x], h2[x], h2[x - 1], ec[x], 16), h2[x])
            yield turn


def plane_tile(fetch, xs):
    tile = (8, 128)
    lead = lax.broadcasted_iota(jnp.int32, tile, 1) - lax.broadcasted_iota(jnp.int32, tile, 0)
    row = lax.broadcasted_iota(jnp.int32, tile, 0)
    out = jnp.zeros(tile, jnp.float32)
    for low in range(8):
        total = jnp.zeros(tile, jnp.float32)
        here = [x for x in xs if x % 8 == low]
        if not here:
            continue
        for x in here:
            for c in range(2):
                for half in range(2):
                    value = jnp.broadcast_to(fetch(c, x, half)[:, 64:65], tile)
                    total = jnp.where(lead == (c * 4 + x // 8) * 16 + half * 8, value, total)
        out = jnp.where(row == low, jnp.sum(total, axis=0, keepdims=True), out)
    return out


def saved_planes(nx):
    return [(0, 0), (1, 1), (2, 1), (0, nx - 2), (1, nx - 2), (2, nx - 3)]


def inner_kernel(e_ref, h_ref, m_ref, p_ref, third_ref, table_ref, eo_hbm, ho_hbm, tile_ref, saved_ref, first_ref, eo_ref, ho_ref, sems):
    refs = (e_ref, h_ref, m_ref, p_ref)
    nx = e_ref.shape[1]

    def planes(x):
        return [jnp.concatenate([field_plane(refs, f, x), third_ref[f, x]], axis=0) for f in ALL]

    def keep_first_step(x, e):
        first_ref[0, x] = e[0][0:16]
        first_ref[1, x] = e[1][0:16]

    copies = []

    def store(x, e, h):
        for c in range(3):
            eo_ref[c, x] = e[c]
            ho_ref[c, x] = h[c][0:16]
        if x + 1 in CUTS:
            start = 2 if x + 1 == CUTS[0] else CUTS[CUTS.index(x + 1) - 1]
            for ref, hbm in ((eo_ref, eo_hbm), (ho_ref, ho_hbm)):
                part = pl.ds(start, x + 1 - start)
                copies.append(pltpu.make_async_copy(ref.at[:, part], hbm.at[:, part], sems.at[len(copies)]))
                copies[-1].start()

    def save(stage, x, value):
        if (stage, x) in saved_planes(nx):
            for c in range(3):
                saved_ref[saved_planes(nx).index((stage, x)), c] = value[c]

    for _ in Window(table_ref).run(planes, 2, nx - 2, keep_first_step, store, SKEW, save=save):
        pass
    for step, ref in enumerate((first_ref, eo_ref)):
        tile_ref[step] = plane_tile(lambda c, x, half: ref[c, x, half * 8:half * 8 + 8, :], range(2, nx - 2))
    for copy in copies:
        copy.wait()


def edge_kernel(e_ref, h_ref, m_ref, p_ref, third_ref, outer_got, inner_got, table_ref, tile_ref, saved_ref, coef_ref,
                eo_ref, ho_ref, part_ref, first_ref, right_ref, left_ref):
    refs = (e_ref, h_ref, m_ref, p_ref)
    nx = e_ref.shape[1]
    second = is_second("gx")

    @pl.when(second == 0)
    def _():
        right_ref[...] = outer_got[...]
        left_ref[...] = inner_got[...]

    @pl.when(second == 1)
    def _():
        right_ref[...] = inner_got[...]
        left_ref[...] = outer_got[...]

    def planes(x):
        return [jnp.concatenate([field_plane(refs, f, x), third_ref[f, x]], axis=0) for f in ALL]

    def slot(x):
        return x if x < 2 else x - nx + 4

    def keep_first_step(x, e):
        first_ref[0, slot(x)] = e[0][0:16]
        first_ref[1, slot(x)] = e[1][0:16]

    def store(x, e, h):
        for c in range(3):
            eo_ref[c, slot(x)] = e[c]
            ho_ref[c, slot(x)] = h[c][0:16]

    window = Window(table_ref)
    held = [tuple(saved_ref[k, c] for c in range(3)) for k in range(6)]
    low_known = ({0: held[0], 1: None, 2: None}, {1: held[1], 2: None}, {1: held[2]})
    high_known = (
        {nx - 4: None, nx - 3: None, nx - 2: held[3]}, {nx - 3: None, nx - 2: held[4]}, {nx - 3: held[5]},
    )
    low = window.run(planes, 0, 2, keep_first_step, store, EDGE_SKEW, behind=right_ref, known=low_known)
    high = window.run(planes, nx - 2, nx, keep_first_step, store, EDGE_SKEW, ahead=left_ref, known=high_known)
    for _ in zip(low, high):
        pass
    tiles = []
    for step, ref in enumerate((first_ref, eo_ref)):
        edge = plane_tile(lambda c, x, half: ref[c, slot(x), half * 8:half * 8 + 8, :], (0, 1, nx - 2, nx - 1))
        tiles.append(tile_ref[step] + edge)
    for s in range(2 * NFREQ):
        first_coef, second_coef = (jnp.broadcast_to(coef_ref[k:k + 1, s:s + 1], (8, 128)) for k in range(2))
        part_ref[s] = first_coef * tiles[0] + second_coef * tiles[1]


def last_kernel(got_ref, ee_ref, he_ref, _e, _h, eo_hbm, ho_hbm, spectra_hbm, out_ref, sems):
    nx = eo_hbm.shape[1]
    pairs = []
    for edge, out in ((ee_ref, eo_hbm), (he_ref, ho_hbm)):
        pairs.append((edge.at[:, 0:2], out.at[:, 0:2]))
        pairs.append((edge.at[:, 2:4], out.at[:, nx - 2:nx]))
    copies = [pltpu.make_async_copy(src, dst, sems.at[i]) for i, (src, dst) in enumerate(pairs)]
    for copy in copies:
        copy.start()
    unpack(got_ref, out_ref)
    copies.append(pltpu.make_async_copy(out_ref, spectra_hbm, sems.at[len(pairs)]))
    copies[-1].start()
    for copy in copies:
        copy.wait()


def unpack(got_ref, out_ref):
    block = lax.broadcasted_iota(jnp.int32, (8, 128), 1) // 16
    for half in range(2):
        v = [got_ref[half * 8 + k] for k in range(8)]
        for bit in range(3):
            by = 1 << bit
            low_block = (block // by) % 2 == 0
            for a in range(8):
                if a & by:
                    continue
                low, high = v[a], v[a + by]
                v[a] = jnp.where(low_block, low, pltpu.roll(high, 16 * by, 1))
                v[a + by] = jnp.where(low_block, pltpu.roll(low, 128 - 16 * by, 1), high)
        for j in range(8):
            out_ref[0, j // 4, (j % 4) * 8:(j % 4) * 8 + 8, half * 128:half * 128 + 128] = v[j]


def shape(*dims):
    return jax.ShapeDtypeStruct(dims, jnp.float32)


SKEW = 1
EDGE_SKEW = 1
CUTS = (10, 18, 26, 30)
VM = pl.BlockSpec(memory_space=pltpu.VMEM)
HBM = pl.BlockSpec(memory_space=pltpu.HBM)
LIMIT = pltpu.CompilerParams(vmem_limit_bytes=16 << 20)


def cost(flops):
    return pl.CostEstimate(flops=flops, bytes_accessed=4 << 20, transcendentals=0)


def local(electric, magnetic, material, pml_flags, permittivity, pml_sigma, omega):
    nx, ny, nz = material.shape
    moments = jnp.arange(1, STEPS + 1, dtype=jnp.float32)[:, None] * time_step
    whole, edge = shape(3, nx, ny, nz), shape(3, 4, ny, nz)

    fields = (electric, magnetic, material, pml_flags)
    inner, outer, table, omega = pl.pallas_call(
        rows_kernel,
        out_shape=(shape(MSG, nx, nz), shape(MSG, nx, nz), shape(16, nz), shape(1, NFREQ)),
        in_specs=[HBM] * 7, out_specs=(VM,) * 4,
        scratch_shapes=[
            pltpu.VMEM((3, nx, nz), jnp.int32), pltpu.VMEM((2, nx, nz), jnp.int32),
            pltpu.VMEM((1, nz), jnp.float32), pltpu.SMEM((NMAT,), jnp.float32), pltpu.SemaphoreType.DMA((17,)),
        ], compiler_params=LIMIT,
    )(*(pltpu.with_memory_space_constraint(a, pltpu.HBM) for a in (*fields, permittivity, pml_sigma[None], omega[None])))
    coef = jnp.concatenate([jnp.cos(omega * moments), -jnp.sin(omega * moments)], axis=1)
    outer, inner = swapped(outer, "gy", 1), gather_inner(inner, "gy")
    inner, outer, third = pl.pallas_call(
        planes_kernel,
        out_shape=(shape(X_MSG, 24, nz), shape(X_MSG, 24, nz), shape(8, nx, 8, nz)),
        in_specs=[VM] * 7, out_specs=(VM,) * 3, compiler_params=LIMIT,
    )(*fields, inner, outer, table)
    outer, inner = swapped(outer, "gx", 1), swapped(inner, "gx", 0)
    ei, hi, tile, saved = pl.pallas_call(
        inner_kernel,
        out_shape=(whole, whole, shape(2, 8, 128), shape(6, 3, 24, nz)),
        in_specs=[VM] * 6, out_specs=(HBM, HBM, VM, VM),
        scratch_shapes=[
            pltpu.VMEM((2, nx, ny, nz), jnp.float32), pltpu.VMEM((3, nx, ny, nz), jnp.float32),
            pltpu.VMEM((3, nx, ny, nz), jnp.float32), pltpu.SemaphoreType.DMA((2 * len(CUTS),)),
        ], compiler_params=LIMIT, cost_estimate=cost(40 << 20),
    )(*fields, third, table)
    ee, he, part = pl.pallas_call(
        edge_kernel,
        out_shape=(edge, edge, shape(2 * NFREQ, 8, 128)),
        in_specs=[VM] * 11, out_specs=(VM,) * 3,
        scratch_shapes=[
            pltpu.VMEM((2, 4, ny, nz), jnp.float32),
            pltpu.VMEM((X_MSG, 24, nz), jnp.float32), pltpu.VMEM((X_MSG, 24, nz), jnp.float32),
        ], compiler_params=LIMIT,
    )(*fields, third, outer, inner, table, tile, saved, coef)
    got = lax.all_to_all(part, "gy", split_axis=0, concat_axis=0, tiled=True)
    electric_out, magnetic_out, spectra = pl.pallas_call(
        last_kernel,
        out_shape=(whole, whole, shape(1, 2, nx, 16 * ny)),
        in_specs=[VM] * 3 + [HBM] * 2, out_specs=(HBM,) * 3, input_output_aliases={3: 0, 4: 1},
        scratch_shapes=[pltpu.VMEM((1, 2, nx, 16 * ny), jnp.float32), pltpu.SemaphoreType.DMA((5,))], compiler_params=LIMIT,
    )(got, ee, he, ei, hi)
    return electric_out, magnetic_out, spectra


def solution(mesh):
    placed = (
        P(None, "gx", "gy", None),
        P(None, "gx", "gy", None),
        P("gx", "gy", None),
        P("gx", "gy", None),
        P(),
        P(),
        P(),
    )
    return jax.shard_map(
        local,
        mesh=mesh,
        in_specs=placed,
        out_specs=(P(None, "gx", "gy", None), P(None, "gx", "gy", None), P("gy", None, "gx", None)),
        check_vma=False,
    )
```
